512 devices in a mesh: row: 16 (over x, y), col: 32 (over z, core).
Axes of the slice: x: 4, y: 4, z: 16, core: 2. Of those that a mesh axis runs over, the one named last changes fastest.
Arguments:
- kron_inverse: float32 [9216, 9216], P('row', 'col'), may hold values from -1 to 13, as said below
- activations: float32 [2, 128, 9216], P(None, None, 'col'), may hold values from -0.125 to 0.125
Outputs:
- updated: float32 [9216, 9216], P('row', 'col')
- gain_blocks: float32 [2, 9216, 128], P(None, ('row', 'col'))
The draws below stay inside these ranges and needn't reach their ends.
Inputs may be any that keep to these rules, and one draw needn't show every extreme that they name: `kron_inverse`: symmetric positive definite, with smallest eigenvalue at least 0.5.
All inputs are finite; a program needn't handle non-finite values.
Results may differ from the reference program's by a relative error of at most 0.0001.
Values sent between devices are 32-bit elements; how exact they have to be, the bound alone decides.
No kernel may reach another device: no remote copies, remote signals or barrier semaphores. Data moves between devices by JAX's collectives and lax.ppermute only.
A program may use at most 64 MiB of HBM per device.

```python
import jax
import jax.numpy as jnp
from jax import lax

ORDER = 9216
BLK = 128
BLOCKS = 2


def draw_kron_inverse(key, part):
    first, second = jax.random.split(jax.random.fold_in(key, 11), 2)
    spread = 0.5 / jnp.sqrt(2.0 * ORDER)
    raw = jax.random.normal(first, (ORDER, ORDER), jnp.float32)
    diagonal = jnp.exp(jax.random.uniform(second, (ORDER,), jnp.float32, jnp.log(2.0), jnp.log(4.0)))
    symmetric = (raw + raw.T) * spread
    return symmetric + jnp.diag(diagonal)


def steps_of(stream_key, dims, cuts, smallest, top_value):
    def one(position, shards_of):
        steps = jax.random.uniform(jax.random.fold_in(jax.random.fold_in(stream_key, 6), position), (shards_of,), jnp.float32, smallest / len(cuts), top_value / len(cuts))
        return jnp.repeat(jnp.exp(steps), dims[position] // shards_of).reshape((-1,) + (1,) * (len(dims) - position - 1))

    level = one(*cuts[0])
    for cut in cuts[1:]:
        level = level * one(*cut)
    return level


def gaussian(own_key, extent, width, most, shards=(), held_as=jnp.bfloat16):
    factor_of = steps_of(own_key, extent, shards, -0.22, 0.18) if shards else 1.0
    result = jax.random.normal(own_key, extent, jnp.float32) * width * factor_of
    return jnp.minimum(jnp.maximum(result, -most), most).astype(held_as)


def setup_inputs(seed: int = 0) -> dict:
    streams_of = jax.random.split(jax.random.key(seed), 3)
    kron_inverse = draw_kron_inverse(jax.random.fold_in(streams_of[2], 71), 0)
    activations = gaussian(streams_of[1], (BLOCKS, BLK, ORDER), (ORDER // 4) ** -0.5, 0.125, ((2, 32),), jnp.float32)
    return dict(kron_inverse=kron_inverse, activations=activations)


highest = lax.Precision.HIGHEST

def reference(kron_inverse, activations):
    current = kron_inverse
    results = []
    for number in range(BLOCKS):
        block_rows = activations[number]
        weighted = jnp.dot(current, block_rows.T, precision=highest)
        system = jnp.eye(BLK, dtype=jnp.float32) + jnp.dot(block_rows, weighted, precision=highest)
        factor = jnp.linalg.cholesky(system)
        gain = jax.scipy.linalg.cho_solve((factor, True), weighted.T).T
        current = current - jnp.dot(gain, weighted.T, precision=highest)
        results.append(gain)
    return (current, jnp.stack(results))
```

```python
import jax
import jax.numpy as jnp
from jax import lax
from jax.sharding import PartitionSpec as P

highest = lax.Precision.HIGHEST


def dot(a, b):
    return jnp.dot(a, b, precision=highest)


def shards(kron_inverse, activations):
    rows, cols = kron_inverse.shape
    blocks, width = activations.shape[:2]
    wide = blocks * width
    planes = lax.axis_size("row")
    devices = lax.axis_size("col")
    depth = devices // 2
    row = lax.axis_index("row")
    col = lax.axis_index("col")
    lines = [[2 * z + k for z in range(depth)] for k in range(2)]
    pairs = [[2 * z, 2 * z + 1] for z in range(depth)]

    def over_core(value):
        return lax.all_to_all(value, "col", 0, 0, tiled=True, axis_index_groups=pairs)

    def over_z(value):
        return lax.all_to_all(value, "col", 0, 0, tiled=True, axis_index_groups=lines)

    def over_plane(value):
        return lax.all_to_all(value, "row", 0, 0, tiled=True)

    def copies(value, count):
        return jnp.broadcast_to(value[None], (count, *value.shape))

    half = rows // 2
    share = half // depth
    slab = wide // planes
    spare = -slab * share % wide
    extra = (slab * share + spare) // wide
    stacked = activations.reshape(wide, cols)
    partial = dot(kron_inverse, stacked.T)
    summed = jnp.sum(over_core(partial.reshape(2, half, wide)), axis=0)
    mine = lax.dynamic_slice_in_dim(stacked, row * slab, slab, 0)
    mine = mine.reshape(slab, depth, share).transpose(1, 0, 2).reshape(depth, slab * share)
    mine = jnp.pad(mine, ((0, 0), (0, spare))).reshape(depth, extra, wide)
    got = over_z(jnp.concatenate([summed.reshape(depth, share, wide), mine], axis=1))
    piece = jnp.sum(got[:, :share], axis=0)
    theirs = got[:, share:].reshape(depth, slab * share + spare)[:, : slab * share]
    theirs = theirs.reshape(depth, slab, share).transpose(1, 0, 2).reshape(slab, depth * share)
    level = over_plane(copies(piece, planes))
    small = dot(theirs, level.reshape(planes * share, wide))
    small = jnp.sum(over_core(small.reshape(2, slab // 2, wide)), axis=0)
    small = jnp.sum(over_z(copies(small, depth)), axis=0)
    terms = over_z(jnp.concatenate([copies(piece, depth), level], axis=1))
    small = over_core(copies(over_plane(copies(small, planes)), 2))
    system = jnp.eye(wide, dtype=jnp.float32) + small.transpose(1, 0, 2, 3).reshape(wide, wide)
    factor = jnp.linalg.cholesky(system)
    inverse = jax.scipy.linalg.solve_triangular(factor, jnp.eye(wide, dtype=jnp.float32), lower=True)
    row_half = terms[:, :share].reshape(half, wide)
    col_terms = terms[:, share:].reshape(half, wide)
    row_terms = over_core(copies(row_half, 2)).reshape(rows, wide)
    row_scaled = dot(row_terms, inverse.T)
    col_scaled = dot(col_terms, inverse.T)
    updated = kron_inverse - dot(row_scaled, col_scaled.T)
    own = rows // devices
    scaled = lax.dynamic_slice_in_dim(row_scaled, col * own, own, 0)
    gains = [
        dot(scaled[:, at : at + width], inverse[at : at + width, at : at + width])
        for at in range(0, wide, width)
    ]
    return updated, jnp.stack(gains)


def solution(mesh):
    return jax.shard_map(
        shards,
        mesh=mesh,
        in_specs=(P("row", "col"), P(None, None, "col")),
        out_specs=(P("row", "col"), P(None, ("row", "col"), None)),
        check_vma=False,
    )
```

```python
import jax
import jax.numpy as jnp
from jax import lax
from jax.experimental import pallas as pl
from jax.experimental.pallas import tpu as pltpu
from jax.sharding import PartitionSpec as P

highest = lax.Precision.HIGHEST
f32 = jnp.float32


def dot(a, b, dims=((1,), (0,))):
    return lax.dot_general(a, b, (dims, ((), ())), precision=highest, preferred_element_type=f32)


def rough(a, b):
    return jnp.dot(a.astype(jnp.bfloat16), b.astype(jnp.bfloat16), preferred_element_type=f32)


def unit(size):
    rows = lax.broadcasted_iota(jnp.int32, (size, size), 0)
    return (rows == lax.broadcasted_iota(jnp.int32, (size, size), 1)).astype(f32)


def invert(block, out_ref, work_ref):
    size = block.shape[0]
    eye = unit(size)
    scale_col = lax.rsqrt(jnp.sum(block * eye, axis=1, keepdims=True))
    scale_row = lax.rsqrt(jnp.sum(block * eye, axis=0, keepdims=True))
    scaled = block * scale_col * scale_row
    off = scaled - eye
    step = jnp.minimum(1.0, 1.9 / (1.0 + jnp.sqrt(jnp.sum(off * off))))
    rest = eye - step * scaled
    guess = eye + rest
    rest = rough(rest, rest)
    for turn in range(3):
        more = rough(guess, rest)
        if turn < 2:
            rest = rough(rest, rest)
        guess = guess + more
    guess = guess * step
    rest = eye - dot(guess, scaled)
    out_ref[...] = guess + rough(rest, guess)
    miss = jnp.sum(rest * rest)

    @pl.when(jnp.logical_not(miss < 1e-2))
    def _():
        work_ref[...] = scaled
        lane = lax.broadcasted_iota(jnp.int32, (1, size), 1)
        line = lax.broadcasted_iota(jnp.int32, (size, 1), 0)

        def sweep(at, carry):
            value = work_ref[...]
            row = work_ref[pl.ds(at, 1), :]
            here = lane == at
            col = jnp.sum(jnp.where(here, value, 0.0), axis=1, keepdims=True)
            pivot = 1.0 / jnp.sum(jnp.where(here, row, 0.0), axis=1, keepdims=True)
            row = jnp.where(here, pivot, row * pivot)
            col = jnp.where(line == at, 0.0, col)
            value = jnp.where(here, 0.0, value)
            work_ref[...] = jnp.where(line == at, row, value - col * row)
            return carry

        lax.fori_loop(0, size, sweep, 0)
        out_ref[...] = work_ref[...]

    guess = out_ref[...]
    rest = eye - dot(guess, scaled)
    out_ref[...] = (guess + rough(rest, guess)) * scale_col * scale_row


def small_kernel(terms_ref, whole_ref, gain_ref, first_ref, last_ref, work_ref):
    wide = terms_ref.shape[0]
    width = wide // 2
    eye = unit(width)
    invert(terms_ref[:width, :width] + eye, first_ref, work_ref)
    first = first_ref[...]
    cross = terms_ref[:width, width:]
    carry = dot(first, cross)
    invert(terms_ref[width:, width:] + eye - dot(cross, carry, ((0,), (0,))), last_ref, work_ref)
    last = last_ref[...]
    corner = dot(carry, last)
    whole_ref[:width, :width] = first + dot(corner, carry, ((1,), (1,)))
    whole_ref[:width, width:] = -corner
    whole_ref[width:, :width] = -corner.T
    whole_ref[width:, width:] = last
    gain_ref[:width, :width] = first
    gain_ref[:width, width:] = -corner
    gain_ref[width:, :width] = jnp.zeros((width, width), f32)
    gain_ref[width:, width:] = last


def small_inverse(terms):
    wide = terms.shape[0]
    return pl.pallas_call(
        small_kernel,
        out_shape=[jax.ShapeDtypeStruct((wide, wide), f32)] * 2,
        scratch_shapes=[pltpu.VMEM((wide // 2, wide // 2), f32)] * 3,
    )(terms)


def shards(kron_inverse, activations):
    rows, cols = kron_inverse.shape
    blocks, width = activations.shape[:2]
    wide = blocks * width
    planes = lax.axis_size("row")
    devices = lax.axis_size("col")
    depth = devices // 2
    row = lax.axis_index("row")
    col = lax.axis_index("col")
    lines = [[2 * z + k for z in range(depth)] for k in range(2)]
    pairs = [[2 * z, 2 * z + 1] for z in range(depth)]

    def over_core(value):
        return lax.all_to_all(value, "col", 0, 0, tiled=True, axis_index_groups=pairs)

    def over_z(value):
        return lax.all_to_all(value, "col", 0, 0, tiled=True, axis_index_groups=lines)

    def over_plane(value):
        return lax.all_to_all(value, "row", 0, 0, tiled=True)

    def copies(value, count):
        return jnp.broadcast_to(value[None], (count, *value.shape))

    half = rows // 2
    share = half // depth
    slab = wide // planes

    def whole(value):
        left = value[:, :share].reshape(half, width)
        return jnp.concatenate([left, value[:, share:].reshape(half, width)], axis=1)

    spare = -slab * share % (4 * width)
    stacked = activations.reshape(wide, cols)
    partial = dot(kron_inverse, stacked.T)
    summed = jnp.sum(over_core(partial.reshape(2, half, wide)), axis=0)
    mine = lax.dynamic_slice_in_dim(stacked, row * slab, slab, 0)
    mine = mine.reshape(slab, depth, share).transpose(1, 0, 2).reshape(depth, slab * share)
    mine = jnp.pad(mine, ((0, 0), (0, spare))).reshape(depth, -1, width)
    parts = [summed[:, at : at + width].reshape(depth, share, width) for at in range(0, wide, width)]
    got = over_z(jnp.concatenate([*parts, mine], axis=1))
    piece = jnp.sum(got[:, : blocks * share], axis=0)
    theirs = got[:, blocks * share :].reshape(depth, slab * share + spare)[:, : slab * share]
    theirs = theirs.reshape(depth, slab, share).transpose(1, 0, 2).reshape(slab, depth * share)
    level = over_plane(copies(piece, planes))
    terms = dot(theirs, whole(level))
    terms = jnp.sum(over_core(terms.reshape(2, slab // 2, wide)), axis=0)
    terms = jnp.concatenate([terms[:, :width], terms[:, width:]], axis=0)
    cut = -(-blocks * share // planes)
    users = blocks * share // cut
    part = lax.dynamic_slice_in_dim(level, jnp.minimum(row, users - 1) * cut, cut, 1)
    line = over_z(jnp.concatenate([copies(terms, depth), copies(piece, depth), part], axis=1))
    terms = jnp.sum(line[:, :slab], axis=0)
    row_half = whole(line[:, slab : slab + blocks * share])
    part = line[:, slab + blocks * share :].reshape(depth * cut, width)
    disc = over_plane(copies(jnp.concatenate([terms, part], axis=0), planes))
    terms = over_core(copies(disc[:, :slab], 2))
    row_terms = over_core(copies(row_half, 2)).reshape(rows, wide)
    col_terms = disc[:users, slab:].reshape(blocks, users // blocks, depth, cut, width)
    col_terms = col_terms.transpose(2, 1, 3, 0, 4).reshape(half, wide)
    terms = terms.reshape(2, planes, blocks, slab // 2, width).transpose(1, 0, 3, 2, 4)
    inverse, gain = small_inverse(terms.reshape(wide, wide))
    scaled = dot(col_terms, inverse)
    updated = kron_inverse - dot(row_terms, scaled, ((1,), (1,)))
    own = rows // devices
    gains = dot(lax.dynamic_slice_in_dim(row_terms, col * own, own, 0), gain)
    return updated, gains.reshape(own, blocks, width).transpose(1, 0, 2)


def solution(mesh):
    return jax.shard_map(
        shards,
        mesh=mesh,
        in_specs=(P("row", "col"), P(None, None, "col")),
        out_specs=(P("row", "col"), P(None, ("row", "col"), None)),
        check_vma=False,
    )
```

```python
import jax
import jax.numpy as jnp
from jax import lax
from jax.experimental import pallas as pl
from jax.experimental.pallas import tpu as pltpu
from jax.sharding import PartitionSpec as P


highest = lax.Precision.HIGHEST
f32 = jnp.float32


def dot(a, b, dims=((1,), (0,))):
    return lax.dot_general(a, b, (dims, ((), ())), precision=highest, preferred_element_type=f32)


def rough(a, b):
    return jnp.dot(a.astype(jnp.bfloat16), b.astype(jnp.bfloat16), preferred_element_type=f32)


def unit(size):
    rows = lax.broadcasted_iota(jnp.int32, (size, size), 0)
    return (rows == lax.broadcasted_iota(jnp.int32, (size, size), 1)).astype(f32)


def invert(block, out_ref, work_ref):
    size = block.shape[0]
    eye = unit(size)
    scale_col = lax.rsqrt(jnp.sum(block * eye, axis=1, keepdims=True))
    scale_row = lax.rsqrt(jnp.sum(block * eye, axis=0, keepdims=True))
    scaled = block * scale_col * scale_row
    off = scaled - eye
    step = jnp.minimum(1.0, 1.9 / (1.0 + jnp.sqrt(jnp.sum(off * off))))
    rest = eye - step * scaled
    guess = eye + rest
    rest = rough(rest, rest)
    for turn in range(3):
        more = rough(guess, rest)
        if turn < 2:
            rest = rough(rest, rest)
        guess = guess + more
    guess = guess * step
    rest = eye - dot(guess, scaled)
    out_ref[...] = guess + rough(rest, guess)
    miss = jnp.sum(rest * rest)

    @pl.when(jnp.logical_not(miss < 1e-2))
    def _():
        work_ref[...] = scaled
        lane = lax.broadcasted_iota(jnp.int32, (1, size), 1)
        line = lax.broadcasted_iota(jnp.int32, (size, 1), 0)

        def sweep(at, carry):
            value = work_ref[...]
            row = work_ref[pl.ds(at, 1), :]
            here = lane == at
            col = jnp.sum(jnp.where(here, value, 0.0), axis=1, keepdims=True)
            pivot = 1.0 / jnp.sum(jnp.where(here, row, 0.0), axis=1, keepdims=True)
            row = jnp.where(here, pivot, row * pivot)
            col = jnp.where(line == at, 0.0, col)
            value = jnp.where(here, 0.0, value)
            work_ref[...] = jnp.where(line == at, row, value - col * row)
            return carry

        lax.fori_loop(0, size, sweep, 0)
        out_ref[...] = work_ref[...]

    guess = out_ref[...]
    rest = eye - dot(guess, scaled)
    out_ref[...] = (guess + rough(rest, guess)) * scale_col * scale_row


def closing_kernel(terms_ref, rows_ref, cols_ref, own_ref, start_ref, out_ref, gain_ref, first_ref, last_ref, work_ref):
    depth = terms_ref.shape[1]
    width = first_ref.shape[0]
    step = terms_ref.shape[2] // 2
    blocks = [[None, None], [None, None]]
    for high in range(2):
        for right in range(2):
            part = terms_ref[:, high * depth // 2 : (high + 1) * depth // 2, right * step : (right + 1) * step]
            blocks[high][right] = jnp.transpose(part, (1, 0, 2, 3)).reshape(width, width)
    eye = unit(width)
    invert(blocks[0][0] + eye, first_ref, work_ref)
    first = first_ref[...]
    cross = blocks[0][1]
    carry = dot(first, cross)
    invert(blocks[1][1] + eye - dot(cross, carry, ((0,), (0,))), last_ref, work_ref)
    last = last_ref[...]
    corner = dot(carry, last)
    whole = first + dot(corner, carry, ((1,), (1,)))
    left, right = cols_ref[:, :width], cols_ref[:, width:]
    left, right = (
        dot(left, whole) - dot(right, corner, ((1,), (1,))),
        dot(right, last) - dot(left, corner),
    )
    out = start_ref[...] - dot(left, rows_ref[:, :width], ((1,), (1,)))
    out_ref[...] = out - dot(right, rows_ref[:, width:], ((1,), (1,)))
    left, right = own_ref[:, :width], own_ref[:, width:]
    gain_ref[:, 0] = dot(left, first)
    gain_ref[:, 1] = dot(right, last) - dot(left, corner)


def closing(terms, row_terms, col_terms, own, start):
    width = own.shape[1] // 2
    return pl.pallas_call(
        closing_kernel,
        out_shape=[
            jax.ShapeDtypeStruct(start.shape, f32),
            jax.ShapeDtypeStruct((own.shape[0], 2, width), f32),
        ],
        in_specs=[pl.BlockSpec(memory_space=pltpu.VMEM)] * 5,
        scratch_shapes=[pltpu.VMEM((width, width), f32)] * 3,
    )(terms, row_terms, col_terms, own, start)


def shards(kron_inverse, activations):
    rows, cols = kron_inverse.shape
    blocks, width = activations.shape[:2]
    wide = blocks * width
    planes = lax.axis_size("row")
    devices = lax.axis_size("col")
    depth = devices // 2
    row = lax.axis_index("row")
    col = lax.axis_index("col")
    lines = [[2 * z + k for z in range(depth)] for k in range(2)]

    def from_partner(value):
        return lax.ppermute(value, "col", [(at, at ^ 1) for at in range(devices)])

    def over_z(value):
        return lax.all_to_all(value, "col", 0, 0, tiled=True, axis_index_groups=lines)

    def over_plane(value):
        return lax.all_to_all(value, "row", 0, 0, tiled=True)

    def copies(value, count):
        return jnp.broadcast_to(value[None], (count, *value.shape))

    half = rows // 2
    share = half // depth
    slab = wide // planes

    def whole(value):
        left = value[:, :share].reshape(half, width)
        return jnp.concatenate([left, value[:, share:].reshape(half, width)], axis=1)

    spare = -slab * share % (4 * width)
    core = col % 2
    partial = jnp.stack([dot(kron_inverse, block.T) for block in activations])
    other = lax.dynamic_slice_in_dim(partial, (1 - core) * half, half, 1)
    summed = lax.dynamic_slice_in_dim(partial, core * half, half, 1) + from_partner(other)
    mine = lax.dynamic_slice_in_dim(activations.reshape(wide, cols), row * slab, slab, 0)
    mine = mine.reshape(slab, depth, share).transpose(1, 0, 2).reshape(depth, slab * share)
    mine = jnp.pad(mine, ((0, 0), (0, spare))).reshape(depth, -1, width)
    parts = [summed[at].reshape(depth, share, width) for at in range(blocks)]
    got = over_z(jnp.concatenate([*parts, mine], axis=1))
    piece = jnp.sum(got[:, : blocks * share], axis=0)
    theirs = got[:, blocks * share :].reshape(depth, slab * share + spare)[:, : slab * share]
    theirs = theirs.reshape(depth, slab, share).transpose(1, 0, 2).reshape(slab, depth * share)
    level = over_plane(copies(piece, planes))
    terms = dot(theirs, whole(level))
    other = lax.dynamic_slice_in_dim(terms, (1 - core) * (slab // 2), slab // 2, 0)
    terms = lax.dynamic_slice_in_dim(terms, core * (slab // 2), slab // 2, 0) + from_partner(other)
    terms = jnp.concatenate([terms[:, :width], terms[:, width:]], axis=0)
    cut = -(-blocks * share // planes)
    users = blocks * share // cut
    part = lax.dynamic_slice_in_dim(level, jnp.minimum(row, users - 1) * cut, cut, 1)
    line = over_z(jnp.concatenate([copies(terms, depth), copies(piece, depth), part], axis=1))
    terms = jnp.sum(line[:, :slab], axis=0)
    row_half = whole(line[:, slab : slab + blocks * share])
    part = line[:, slab + blocks * share :].reshape(depth * cut, width)
    disc = over_plane(copies(jnp.concatenate([terms, part], axis=0), planes))
    row_other = from_partner(row_half)

    def in_order(value, other):
        low = jnp.where(core == 0, value, other)
        return jnp.stack([low, jnp.where(core == 0, other, value)])

    row_terms = in_order(row_half, row_other).reshape(rows, wide)
    own = rows // devices
    own_terms = lax.dynamic_slice_in_dim(row_terms, col * own, own, 0)
    terms = disc[:, :slab]
    terms = in_order(terms, from_partner(terms))
    col_terms = disc[:users, slab:].reshape(blocks, users // blocks, depth, cut, width)
    col_terms = col_terms.transpose(2, 1, 3, 0, 4).reshape(half, wide)
    updated, gains = closing(terms, row_terms, col_terms, own_terms, kron_inverse.T)
    return updated.T, gains.transpose(1, 0, 2)


def solution(mesh):
    return jax.shard_map(
        shards,
        mesh=mesh,
        in_specs=(P("row", "col"), P(None, None, "col")),
        out_specs=(P("row", "col"), P(None, ("row", "col"), None)),
        check_vma=False,
    )
```

```python
import jax
import jax.numpy as jnp
from jax import lax
from jax.experimental import pallas as pl
from jax.experimental.pallas import tpu as pltpu
from jax.sharding import PartitionSpec as P


highest = lax.Precision.HIGHEST
f32 = jnp.float32


def dot(a, b, dims=((1,), (0,))):
    return lax.dot_general(a, b, (dims, ((), ())), precision=highest, preferred_element_type=f32)


def rough(a, b):
    return jnp.dot(a.astype(jnp.bfloat16), b.astype(jnp.bfloat16), preferred_element_type=f32)


def unit(size):
    rows = lax.broadcasted_iota(jnp.int32, (size, size), 0)
    return (rows == lax.broadcasted_iota(jnp.int32, (size, size), 1)).astype(f32)


def invert(block, out_ref, work_ref):
    size = block.shape[0]
    eye = unit(size)
    scale_col = lax.rsqrt(jnp.sum(block * eye, axis=1, keepdims=True))
    scale_row = lax.rsqrt(jnp.sum(block * eye, axis=0, keepdims=True))
    scaled = block * scale_col * scale_row
    off = scaled - eye
    step = jnp.minimum(1.0, 1.9 / (1.0 + jnp.sqrt(jnp.sum(off * off))))
    rest = eye - step * scaled
    guess = eye + rest
    rest = rough(rest, rest)
    for turn in range(3):
        more = rough(guess, rest)
        if turn < 2:
            rest = rough(rest, rest)
        guess = guess + more
    guess = guess * step
    rest = eye - dot(guess, scaled)
    out_ref[...] = guess + rough(rest, guess)
    miss = jnp.sum(rest * rest)

    @pl.when(jnp.logical_not(miss < 1e-2))
    def _():
        work_ref[...] = scaled
        lane = lax.broadcasted_iota(jnp.int32, (1, size), 1)
        line = lax.broadcasted_iota(jnp.int32, (size, 1), 0)

        def sweep(at, carry):
            value = work_ref[...]
            row = work_ref[pl.ds(at, 1), :]
            here = lane == at
            col = jnp.sum(jnp.where(here, value, 0.0), axis=1, keepdims=True)
            pivot = 1.0 / jnp.sum(jnp.where(here, row, 0.0), axis=1, keepdims=True)
            row = jnp.where(here, pivot, row * pivot)
            col = jnp.where(line == at, 0.0, col)
            value = jnp.where(here, 0.0, value)
            work_ref[...] = jnp.where(line == at, row, value - col * row)
            return carry

        lax.fori_loop(0, size, sweep, 0)
        out_ref[...] = work_ref[...]

    guess = out_ref[...]
    rest = eye - dot(guess, scaled)
    out_ref[...] = (guess + rough(rest, guess)) * scale_col * scale_row


def opening_kernel(core_ref, start_ref, lines_ref, keep_ref, send_ref):
    blocks, half, width = keep_ref.shape
    lines = jnp.concatenate([lines_ref[at] for at in range(blocks)], axis=1)
    value = dot(start_ref[...], lines, ((0,), (0,)))

    def store(low_ref, high_ref):
        for at in range(blocks):
            low_ref[at] = value[:half, at * width : (at + 1) * width]
            high_ref[at] = value[half:, at * width : (at + 1) * width]

    pl.when(core_ref[0] == 0)(lambda: store(keep_ref, send_ref))
    pl.when(core_ref[0] != 0)(lambda: store(send_ref, keep_ref))


def opening(core, start, lines):
    blocks, _, width = lines.shape
    in_vmem = pl.BlockSpec(memory_space=pltpu.VMEM)
    return pl.pallas_call(
        opening_kernel,
        out_shape=[pltpu.VMEM((blocks, start.shape[1] // 2, width), f32)] * 2,
        in_specs=[pl.BlockSpec(memory_space=pltpu.SMEM), in_vmem, in_vmem],
    )(core.reshape(1), start, lines)


def closing_kernel(terms_ref, rows_ref, cols_ref, own_ref, start_ref, out_ref, gain_ref, first_ref, last_ref, work_ref):
    depth = terms_ref.shape[1]
    width = first_ref.shape[0]
    step = terms_ref.shape[2] // 2
    blocks = [[None, None], [None, None]]
    for high in range(2):
        for right in range(2):
            part = terms_ref[:, high * depth // 2 : (high + 1) * depth // 2, right * step : (right + 1) * step]
            blocks[high][right] = jnp.transpose(part, (1, 0, 2, 3)).reshape(width, width)
    eye = unit(width)
    invert(blocks[0][0] + eye, first_ref, work_ref)
    first = first_ref[...]
    cross = blocks[0][1]
    carry = dot(first, cross)
    invert(blocks[1][1] + eye - dot(cross, carry, ((0,), (0,))), last_ref, work_ref)
    last = last_ref[...]
    corner = dot(carry, last)
    whole = first + dot(corner, carry, ((1,), (1,)))
    left, right = cols_ref[:, :width], cols_ref[:, width:]
    left, right = (
        dot(left, whole) - dot(right, corner, ((1,), (1,))),
        dot(right, last) - dot(left, corner),
    )
    out = start_ref[...] - dot(left, rows_ref[:, :width], ((1,), (1,)))
    out_ref[...] = out - dot(right, rows_ref[:, width:], ((1,), (1,)))
    left, right = own_ref[:, :width], own_ref[:, width:]
    gain_ref[:, 0] = dot(left, first)
    gain_ref[:, 1] = dot(right, last) - dot(left, corner)


def closing(terms, row_terms, col_terms, own, start):
    width = own.shape[1] // 2
    return pl.pallas_call(
        closing_kernel,
        out_shape=[
            jax.ShapeDtypeStruct(start.shape, f32),
            jax.ShapeDtypeStruct((own.shape[0], 2, width), f32),
        ],
        in_specs=[pl.BlockSpec(memory_space=pltpu.VMEM)] * 5,
        scratch_shapes=[pltpu.VMEM((width, width), f32)] * 3,
    )(*(pltpu.with_memory_space_constraint(x, pltpu.VMEM) for x in (terms, row_terms, col_terms, own)), start)


def shards(kron_inverse, activations):
    rows, cols = kron_inverse.shape
    blocks, width = activations.shape[:2]
    wide = blocks * width
    planes = lax.axis_size("row")
    devices = lax.axis_size("col")
    depth = devices // 2
    row = lax.axis_index("row")
    col = lax.axis_index("col")
    near = 4 if depth % 4 == 0 else 1
    far = depth // near
    lines = [[2 * z + k for z in range(depth)] for k in range(2)]
    close = [[2 * (near * j + q) + k for q in range(near)] for j in range(far) for k in range(2)]
    apart = [[2 * (near * j + q) + k for j in range(far)] for q in range(near) for k in range(2)]

    def from_partner(value):
        return lax.ppermute(value, "col", [(at, at ^ 1) for at in range(devices)])

    def over_z(value, groups):
        return lax.all_to_all(value, "col", 0, 0, tiled=True, axis_index_groups=groups)

    def over_plane(value):
        return lax.all_to_all(value, "row", 0, 0, tiled=True)

    def copies(value, count):
        return jnp.broadcast_to(value[None], (count, *value.shape))

    half = rows // 2
    share = half // depth
    slab = wide // planes

    def whole(value):
        left = value[:, :share].reshape(half, width)
        return jnp.concatenate([left, value[:, share:].reshape(half, width)], axis=1)

    spare = -slab * share % (4 * width)
    core = col % 2
    keep, send = opening(core, kron_inverse.T, activations.transpose(0, 2, 1))
    summed = keep + from_partner(send)
    mine = lax.dynamic_slice_in_dim(activations.reshape(wide, cols), row * slab, slab, 0)
    mine = mine.reshape(slab, depth, share).transpose(1, 0, 2).reshape(depth, slab * share)
    mine = jnp.pad(mine, ((0, 0), (0, spare))).reshape(depth, -1, width)
    parts = [summed[at].reshape(depth, share, width) for at in range(blocks)]
    got = over_z(jnp.concatenate([*parts, mine], axis=1), lines)
    piece = jnp.sum(got[:, : blocks * share], axis=0)
    theirs = got[:, blocks * share :].reshape(depth, slab * share + spare)[:, : slab * share]
    theirs = theirs.reshape(depth, slab, share).transpose(1, 0, 2).reshape(slab, depth * share)
    level = over_plane(copies(piece, planes))
    terms = dot(theirs, whole(level))
    other = lax.dynamic_slice_in_dim(terms, (1 - core) * (slab // 2), slab // 2, 0)
    terms = lax.dynamic_slice_in_dim(terms, core * (slab // 2), slab // 2, 0) + from_partner(other)
    terms = jnp.concatenate([terms[:, :width], terms[:, width:]], axis=0)
    cut = -(-blocks * share // planes)
    users = blocks * share // cut
    part = lax.dynamic_slice_in_dim(level, jnp.minimum(row, users - 1) * cut, cut, 1)
    held = blocks * share

    def padded(value):
        return jnp.pad(value, ((0, 0), (0, -value.shape[1] % 8), (0, 0)))

    part = padded(part.reshape(far, near * cut, width))
    there = over_z(jnp.concatenate([copies(terms, far), padded(copies(piece, far)), part], axis=1), apart)
    terms = jnp.sum(there[:, :slab], axis=0)
    tall = held + -held % 8
    pieces = there[:, slab : slab + tall].reshape(far * tall, width)
    part = there[:, slab + tall : slab + tall + near * cut].reshape(far, near, cut, width)
    part = padded(part.transpose(1, 0, 2, 3).reshape(near, far * cut, width))
    there = over_z(jnp.concatenate([copies(terms, near), copies(pieces, near), part], axis=1), close)
    terms = jnp.sum(there[:, :slab], axis=0)
    pieces = there[:, slab : slab + far * tall].reshape(near, far, tall, width).transpose(1, 0, 2, 3)
    row_half = whole(pieces.reshape(depth, tall, width)[:, :held])
    part = there[:, slab + far * tall :][:, : far * cut].reshape(near, far, cut, width)
    part = part.transpose(1, 0, 2, 3).reshape(depth * cut, width)
    disc = over_plane(copies(jnp.concatenate([terms, part], axis=0), planes))
    row_other = from_partner(row_half)

    def in_order(value, other):
        low = jnp.where(core == 0, value, other)
        return jnp.stack([low, jnp.where(core == 0, other, value)])

    row_terms = in_order(row_half, row_other).reshape(rows, wide)
    own = rows // devices
    own_terms = lax.dynamic_slice_in_dim(row_terms, col * own, own, 0)
    terms = disc[:, :slab]
    terms = in_order(terms, from_partner(terms))
    col_terms = disc[:users, slab:].reshape(blocks, users // blocks, depth, cut, width)
    col_terms = col_terms.transpose(2, 1, 3, 0, 4).reshape(half, wide)
    updated, gains = closing(terms, row_terms, col_terms, own_terms, kron_inverse.T)
    return updated.T, gains.transpose(1, 0, 2)


def solution(mesh):
    return jax.shard_map(
        shards,
        mesh=mesh,
        in_specs=(P("row", "col"), P(None, None, "col")),
        out_specs=(P("row", "col"), P(None, ("row", "col"), None)),
        check_vma=False,
    )
```

```python
import jax
import jax.numpy as jnp
from jax import lax
from jax.experimental import pallas as pl
from jax.experimental.pallas import tpu as pltpu
from jax.sharding import PartitionSpec as P


highest = lax.Precision.HIGHEST
f32 = jnp.float32


def dot(a, b, dims=((1,), (0,))):
    return lax.dot_general(a, b, (dims, ((), ())), precision=highest, preferred_element_type=f32)


def rough(a, b):
    return jnp.dot(a.astype(jnp.bfloat16), b.astype(jnp.bfloat16), preferred_element_type=f32)


def unit(size):
    rows = lax.broadcasted_iota(jnp.int32, (size, size), 0)
    return (rows == lax.broadcasted_iota(jnp.int32, (size, size), 1)).astype(f32)


def expanded(block):
    eye = unit(block.shape[0])
    scale_col = lax.rsqrt(jnp.sum(block * eye, axis=1, keepdims=True))
    scale_row = lax.rsqrt(jnp.sum(block * eye, axis=0, keepdims=True))
    scaled = block * scale_col * scale_row
    off = scaled - eye
    step = jnp.minimum(1.0, 1.9 / (1.0 + jnp.sqrt(jnp.sum(off * off))))
    rest = eye - step * scaled
    guess = eye + rest
    rest = rough(rest, rest)
    for turn in range(3):
        more = rough(guess, rest)
        if turn < 2:
            rest = rough(rest, rest)
        guess = guess + more
    guess = guess * step
    rest = eye - dot(guess, scaled)
    miss = jnp.sum(rest * rest)
    guess = guess + rough(rest, guess)
    rest = eye - dot(guess, scaled)
    return (guess + rough(rest, guess)) * scale_col * scale_row, miss


def eliminated(block, work_ref):
    size = block.shape[0]
    lane = lax.broadcasted_iota(jnp.int32, (1, size), 1)
    line = lax.broadcasted_iota(jnp.int32, (size, 1), 0)
    work_ref[...] = block

    def sweep(at, carry):
        value = work_ref[...]
        row = work_ref[pl.ds(at, 1), :]
        here = lane == at
        col = jnp.sum(jnp.where(here, value, 0.0), axis=1, keepdims=True)
        pivot = 1.0 / jnp.sum(jnp.where(here, row, 0.0), axis=1, keepdims=True)
        row = jnp.where(here, pivot, row * pivot)
        col = jnp.where(line == at, 0.0, col)
        value = jnp.where(here, 0.0, value)
        work_ref[...] = jnp.where(line == at, row, value - col * row)
        return carry

    lax.fori_loop(0, size, sweep, 0)
    guess = work_ref[...]
    return guess + dot(unit(size) - dot(guess, block), guess)


def opening_kernel(core_ref, start_ref, lines_ref, keep_ref, send_ref):
    blocks, half, width = keep_ref.shape
    lines = jnp.concatenate([lines_ref[at] for at in range(blocks)], axis=1)
    value = dot(start_ref[...], lines, ((0,), (0,)))

    def store(low_ref, high_ref):
        for at in range(blocks):
            low_ref[at] = value[:half, at * width : (at + 1) * width]
            high_ref[at] = value[half:, at * width : (at + 1) * width]

    pl.when(core_ref[0] == 0)(lambda: store(keep_ref, send_ref))
    pl.when(core_ref[0] != 0)(lambda: store(send_ref, keep_ref))


def opening(core, start, lines):
    blocks, _, width = lines.shape
    in_vmem = pl.BlockSpec(memory_space=pltpu.VMEM)
    return pl.pallas_call(
        opening_kernel,
        out_shape=[pltpu.VMEM((blocks, start.shape[1] // 2, width), f32)] * 2,
        in_specs=[pl.BlockSpec(memory_space=pltpu.SMEM), in_vmem, in_vmem],
    )(core.reshape(1), start, lines)


def closing_kernel(terms_ref, rows_ref, cols_ref, own_ref, start_ref, out_ref, gain_ref, work_ref):
    depth = terms_ref.shape[1]
    step = terms_ref.shape[2] // 2
    width = work_ref.shape[0]

    def block(high, right):
        part = terms_ref[:, high * depth // 2 : (high + 1) * depth // 2, right * step : (right + 1) * step]
        return jnp.transpose(part, (1, 0, 2, 3)).reshape(width, width)

    def solve(inverse):
        first, miss = inverse(block(0, 0) + unit(width))
        cross = block(0, 1)
        carry = dot(first, cross)
        last, more = inverse(block(1, 1) + unit(width) - dot(cross, carry, ((0,), (0,))))
        both = jnp.concatenate([first, carry], axis=1)

        def gains(ref):
            value = dot(ref[:, :width], both)
            return value[:, :width], dot(ref[:, width:] - value[:, width:], last)

        gain_ref[:, 0], gain_ref[:, 1] = gains(own_ref)
        low, high = gains(cols_ref)
        low = low - dot(high, carry, ((1,), (1,)))
        out_ref[...] = start_ref[...] - dot(jnp.concatenate([low, high], axis=1), rows_ref[...], ((1,), (1,)))
        return miss + more

    miss = solve(expanded)

    @pl.when(jnp.logical_not(miss < 1e-2))
    def _():
        solve(lambda value: (eliminated(value, work_ref), 0.0))


def closing(*operands):
    own, start = operands[3:]
    width = own.shape[1] // 2
    in_vmem = pl.BlockSpec(memory_space=pltpu.VMEM)
    return pl.pallas_call(
        closing_kernel,
        out_shape=[
            jax.ShapeDtypeStruct(start.shape, f32),
            jax.ShapeDtypeStruct((own.shape[0], 2, width), f32),
        ],
        in_specs=[in_vmem] * len(operands),
        scratch_shapes=[pltpu.VMEM((width, width), f32)],
    )(*(pltpu.with_memory_space_constraint(x, pltpu.VMEM) for x in operands))


def shards(kron_inverse, activations):
    rows, cols = kron_inverse.shape
    blocks, width = activations.shape[:2]
    wide = blocks * width
    planes = lax.axis_size("row")
    devices = lax.axis_size("col")
    depth = devices // 2
    row = lax.axis_index("row")
    col = lax.axis_index("col")
    lines = [[2 * z + k for z in range(depth)] for k in range(2)]

    def from_partner(value):
        return lax.ppermute(value, "col", [(at, at ^ 1) for at in range(devices)])

    def over_z(value):
        return lax.all_to_all(value, "col", 0, 0, tiled=True, axis_index_groups=lines)

    def over_plane(value):
        return lax.all_to_all(value, "row", 0, 0, tiled=True)

    def copies(value, count):
        return jnp.broadcast_to(value[None], (count, *value.shape))

    half = rows // 2
    share = half // depth
    slab = wide // planes

    def whole(value):
        left = value[:, :share].reshape(half, width)
        return jnp.concatenate([left, value[:, share:].reshape(half, width)], axis=1)

    spare = -slab * share % (4 * width)
    core = col % 2
    keep, send = opening(core, kron_inverse.T, activations.transpose(0, 2, 1))
    summed = keep + from_partner(send)
    mine = lax.dynamic_slice_in_dim(activations.reshape(wide, cols), row * slab, slab, 0)
    mine = mine.reshape(slab, depth, share).transpose(1, 0, 2).reshape(depth, slab * share)
    mine = jnp.pad(mine, ((0, 0), (0, spare))).reshape(depth, -1, width)
    parts = [summed[at].reshape(depth, share, width) for at in range(blocks)]
    got = over_z(jnp.concatenate([*parts, mine], axis=1))
    piece = jnp.sum(got[:, : blocks * share], axis=0)
    theirs = got[:, blocks * share :].reshape(depth, slab * share + spare)[:, : slab * share]
    theirs = theirs.reshape(depth, slab, share).transpose(1, 0, 2).reshape(slab, depth * share)
    again = lax.optimization_barrier(piece)
    level = over_plane(copies(piece, planes))
    terms = dot(theirs, whole(level))
    other = lax.dynamic_slice_in_dim(terms, (1 - core) * (slab // 2), slab // 2, 0)
    terms = lax.dynamic_slice_in_dim(terms, core * (slab // 2), slab // 2, 0) + from_partner(other)
    terms = jnp.concatenate([terms[:, :width], terms[:, width:]], axis=0)
    cut = -(-blocks * share // planes)
    users = blocks * share // cut
    part = lax.dynamic_slice_in_dim(level, jnp.minimum(row, users - 1) * cut, cut, 1)
    line = over_z(jnp.concatenate([copies(terms, depth), copies(again, depth), part], axis=1))
    terms = jnp.sum(line[:, :slab], axis=0)
    row_half = whole(line[:, slab : slab + blocks * share])
    part = line[:, slab + blocks * share :].reshape(depth * cut, width)
    disc = over_plane(copies(jnp.concatenate([terms, part], axis=0), planes))
    row_other = from_partner(row_half)

    def in_order(value, other):
        low = jnp.where(core == 0, value, other)
        return jnp.stack([low, jnp.where(core == 0, other, value)])

    row_terms = in_order(row_half, row_other).reshape(rows, wide)
    own = rows // devices
    own_terms = lax.dynamic_slice_in_dim(row_terms, col * own, own, 0)
    terms = disc[:, :slab]
    terms = in_order(terms, from_partner(terms))
    col_terms = disc[:users, slab:].reshape(blocks, users // blocks, depth, cut, width)
    col_terms = col_terms.transpose(2, 1, 3, 0, 4).reshape(half, wide)
    updated, gains = closing(terms, row_terms, col_terms, own_terms, kron_inverse.T)
    return updated.T, gains.transpose(1, 0, 2)


def solution(mesh):
    return jax.shard_map(
        shards,
        mesh=mesh,
        in_specs=(P("row", "col"), P(None, None, "col")),
        out_specs=(P("row", "col"), P(None, ("row", "col"), None)),
        check_vma=False,
    )
```

```python
import jax
import jax.numpy as jnp
from jax import lax
from jax.experimental import pallas as pl
from jax.experimental.pallas import tpu as pltpu
from jax.sharding import PartitionSpec as P


highest = lax.Precision.HIGHEST
f32 = jnp.float32


def dot(a, b, dims=((1,), (0,))):
    return lax.dot_general(a, b, (dims, ((), ())), precision=highest, preferred_element_type=f32)


def rough(a, b):
    return jnp.dot(a.astype(jnp.bfloat16), b.astype(jnp.bfloat16), preferred_element_type=f32)


def unit(size):
    rows = lax.broadcasted_iota(jnp.int32, (size, size), 0)
    return (rows == lax.broadcasted_iota(jnp.int32, (size, size), 1)).astype(f32)


def expanded(block):
    eye = unit(block.shape[0])
    scale_col = lax.rsqrt(jnp.sum(block * eye, axis=1, keepdims=True))
    scale_row = lax.rsqrt(jnp.sum(block * eye, axis=0, keepdims=True))
    scaled = block * scale_col * scale_row
    off = scaled - eye
    step = jnp.minimum(1.0, 1.9 / (1.0 + jnp.sqrt(jnp.sum(off * off))))
    rest = eye - step * scaled
    guess = eye + rest
    rest = rough(rest, rest)
    for turn in range(3):
        more = rough(guess, rest)
        if turn < 2:
            rest = rough(rest, rest)
        guess = guess + more
    guess = guess * step
    rest = eye - dot(guess, scaled)
    miss = jnp.sum(rest * rest)
    guess = guess + rough(rest, guess)
    rest = eye - dot(guess, scaled)
    return (guess + rough(rest, guess)) * scale_col * scale_row, miss


def eliminated(block, work_ref):
    size = block.shape[0]
    lane = lax.broadcasted_iota(jnp.int32, (1, size), 1)
    line = lax.broadcasted_iota(jnp.int32, (size, 1), 0)
    work_ref[...] = block

    def sweep(at, carry):
        value = work_ref[...]
        row = work_ref[pl.ds(at, 1), :]
        here = lane == at
        col = jnp.sum(jnp.where(here, value, 0.0), axis=1, keepdims=True)
        pivot = 1.0 / jnp.sum(jnp.where(here, row, 0.0), axis=1, keepdims=True)
        row = jnp.where(here, pivot, row * pivot)
        col = jnp.where(line == at, 0.0, col)
        value = jnp.where(here, 0.0, value)
        work_ref[...] = jnp.where(line == at, row, value - col * row)
        return carry

    lax.fori_loop(0, size, sweep, 0)
    guess = work_ref[...]
    return guess + dot(unit(size) - dot(guess, block), guess)


def opening_kernel(core_ref, start_ref, lines_ref, keep_ref, send_ref):
    blocks, half, width = keep_ref.shape
    lines = jnp.concatenate([lines_ref[at] for at in range(blocks)], axis=1)
    value = dot(start_ref[...], lines, ((0,), (0,)))

    def store(low_ref, high_ref):
        for at in range(blocks):
            low_ref[at] = value[:half, at * width : (at + 1) * width]
            high_ref[at] = value[half:, at * width : (at + 1) * width]

    pl.when(core_ref[0] == 0)(lambda: store(keep_ref, send_ref))
    pl.when(core_ref[0] != 0)(lambda: store(send_ref, keep_ref))


def opening(core, start, lines):
    blocks, _, width = lines.shape
    in_vmem = pl.BlockSpec(memory_space=pltpu.VMEM)
    return pl.pallas_call(
        opening_kernel,
        out_shape=[pltpu.VMEM((blocks, start.shape[1] // 2, width), f32)] * 2,
        in_specs=[pl.BlockSpec(memory_space=pltpu.SMEM), in_vmem, in_vmem],
    )(core.reshape(1), start, lines)


def spread_kernel(got_ref, out_ref):
    piece = jnp.sum(got_ref[:, : out_ref.shape[1]], axis=0)
    for at in range(out_ref.shape[0]):
        out_ref[at] = piece


def spread(got, planes, held):
    return pl.pallas_call(
        spread_kernel,
        out_shape=pltpu.VMEM((planes, held, got.shape[2]), f32),
        in_specs=[pl.BlockSpec(memory_space=pltpu.VMEM)],
    )(pltpu.with_memory_space_constraint(got, pltpu.VMEM))


def slab_kernel(row_ref, got_ref, level_ref, send_ref, right_ref):
    depth, held, width = level_ref.shape
    share = held // 2
    tall = right_ref.shape[1]
    row = row_ref[0]
    slab = 2 * width // depth
    groups = width // slab
    packed = got_ref[:, held : held + tall // groups, :]
    packed = jnp.broadcast_to(packed[:, :, None, :], (depth, tall // groups, groups, width))
    packed = pltpu.roll(packed.reshape(depth * tall, width), slab, 1, stride=slab, stride_axis=0)
    right_ref[...] = jnp.zeros(right_ref.shape, f32)
    right_ref[:, :share, :width] = level_ref[:, :share, :]
    right_ref[:, :share, width:] = level_ref[:, share:, :]
    terms = dot(packed[:, :slab], right_ref[...].reshape(depth * tall, 2 * width), ((0,), (0,)))
    terms = pltpu.roll(terms, jnp.where(row == 0, 0, 2 * width - slab * row), 1)
    lane = lax.broadcasted_iota(jnp.int32, (slab, width), 1)
    block = jnp.where(lane < slab, terms[:, width:], 0.0)
    turned = jnp.concatenate([block, jnp.zeros((width - slab, width), f32)], axis=0).T
    block = jnp.where(row < depth // 2, block[: slab // 2], turned[slab // 2 : slab])
    block = jnp.concatenate([block[at : at + 1] for at in reversed(range(slab // 2))], axis=0)
    block = jnp.sum(pltpu.roll(block, 0, 1, stride=slab, stride_axis=0), axis=0, keepdims=True)
    piece = level_ref[row]
    cut = send_ref.shape[1] - slab - held - 1
    part = level_ref[:, pl.ds(jnp.minimum(row, held // cut - 1) * cut, cut), :]
    for at in range(depth):
        send_ref[at, :slab] = terms[:, :width]
        send_ref[at, slab : slab + held] = piece
        send_ref[at, slab + held : slab + held + cut] = part[at]
        send_ref[at, slab + held + cut :] = block


def slab_terms(row, got, level, cut):
    depth, held, width = level.shape
    slab = 2 * width // depth
    tall = -(-held // 2 // 8) * 8
    in_vmem = pl.BlockSpec(memory_space=pltpu.VMEM)
    return pl.pallas_call(
        slab_kernel,
        out_shape=pltpu.VMEM((depth, slab + held + cut + 1, width), f32),
        in_specs=[pl.BlockSpec(memory_space=pltpu.SMEM), in_vmem, in_vmem],
        scratch_shapes=[pltpu.VMEM((depth, tall, 2 * width), f32)],
    )(row.reshape(1), *(pltpu.with_memory_space_constraint(x, pltpu.VMEM) for x in (got, level)))


def closing_kernel(mine_ref, other_ref, rows_ref, cols_ref, own_ref, start_ref, out_ref, gain_ref, work_ref):
    width = work_ref.shape[0]
    slab = mine_ref.shape[0] - 2 * width
    groups = width // slab
    terms = mine_ref[...] + other_ref[...]

    far = [terms[2 * width + n + m : 2 * width + n + m + 1] for n in range(groups) for m in (0, groups)]
    far = jnp.concatenate([jnp.broadcast_to(part, (slab // 2, width)) for part in far], axis=0)
    far = pltpu.roll(far, slab, 1, stride=slab, stride_axis=0)

    def stepped(value):
        parts = [value[n * slab : (n + 1) * slab] for n in range(groups)]
        return jnp.concatenate([pltpu.roll(part, n * slab, 1) if n else part for n, part in enumerate(parts)], axis=0)

    across = lax.broadcasted_iota(jnp.int32, (width, width), 1) // slab
    down = lax.broadcasted_iota(jnp.int32, (width, width), 0) // slab
    upper, lower, far = stepped(terms[:width]), stepped(terms[width : 2 * width]), stepped(far)
    upper_turned, lower_turned = upper.T, lower.T
    cross = jnp.where(across < down, upper, jnp.where(across > down, lower_turned, far))
    upper = jnp.where(across >= down, upper, upper_turned) + unit(width)
    lower = jnp.where(across >= down, lower, lower_turned) + unit(width)

    def solve(inverse):
        first, miss = inverse(upper)
        carry = dot(first, cross)
        last, more = inverse(lower - dot(cross, carry, ((0,), (0,))))
        both = jnp.concatenate([first, carry], axis=1)

        def gains(ref):
            value = dot(ref[:, :width], both)
            return value[:, :width], dot(ref[:, width:] - value[:, width:], last)

        gain_ref[:, 0], gain_ref[:, 1] = gains(own_ref)
        low, high = gains(cols_ref)
        low = low - dot(high, carry, ((1,), (1,)))
        out_ref[...] = start_ref[...] - dot(jnp.concatenate([low, high], axis=1), rows_ref[...], ((1,), (1,)))
        return miss + more

    miss = solve(expanded)

    @pl.when(jnp.logical_not(miss < 1e-2))
    def _():
        solve(lambda value: (eliminated(value, work_ref), 0.0))


def closing(*operands):
    own, start = operands[4:]
    width = own.shape[1] // 2
    in_vmem = pl.BlockSpec(memory_space=pltpu.VMEM)
    return pl.pallas_call(
        closing_kernel,
        out_shape=[
            jax.ShapeDtypeStruct(start.shape, f32),
            jax.ShapeDtypeStruct((own.shape[0], 2, width), f32),
        ],
        in_specs=[in_vmem] * len(operands),
        scratch_shapes=[pltpu.VMEM((width, width), f32)],
    )(*(pltpu.with_memory_space_constraint(x, pltpu.VMEM) for x in operands))


def shards(kron_inverse, activations):
    rows, cols = kron_inverse.shape
    blocks, width = activations.shape[:2]
    wide = blocks * width
    planes = lax.axis_size("row")
    devices = lax.axis_size("col")
    depth = devices // 2
    row = lax.axis_index("row")
    col = lax.axis_index("col")
    lines = [[2 * z + k for z in range(depth)] for k in range(2)]

    def from_partner(value):
        return lax.ppermute(value, "col", [(at, at ^ 1) for at in range(devices)])

    def over_z(value):
        return lax.all_to_all(value, "col", 0, 0, tiled=True, axis_index_groups=lines)

    def over_plane(value):
        return lax.all_to_all(value, "row", 0, 0, tiled=True)

    def copies(value, count):
        return jnp.broadcast_to(value[None], (count, *value.shape))

    half = rows // 2
    share = half // depth
    slab = wide // planes

    def whole(value):
        left = value[:, :share].reshape(half, width)
        return jnp.concatenate([left, value[:, share:].reshape(half, width)], axis=1)

    core = col % 2
    turned = activations.transpose(0, 2, 1)
    keep, send = opening(core, kron_inverse.T, turned)
    summed = keep + from_partner(send)
    groups = width // slab
    mine = lax.dynamic_slice(turned, (row // groups, 0, row % groups * slab), (1, cols, slab))
    mine = jnp.pad(mine.reshape(depth, share, slab), ((0, 0), (0, -share % groups), (0, 0)))
    mine = jnp.flip(mine.reshape(depth, -1, groups, slab), 2).reshape(depth, -1, width)
    parts = [summed[at].reshape(depth, share, width) for at in range(blocks)]
    got = over_z(jnp.concatenate([*parts, mine], axis=1))
    held = blocks * share
    level = over_plane(spread(got, planes, held))
    cut = -(-held // planes)
    users = held // cut
    line = over_z(slab_terms(row, got, level, cut))
    row_half = whole(line[:, slab : slab + held])
    terms = jnp.sum(line[:, :slab], axis=0)
    far = jnp.sum(line[:, slab + held + cut :], axis=0)
    part = line[:, slab + held : slab + held + cut].reshape(depth * cut, width)
    disc = over_plane(copies(jnp.concatenate([terms, part, far], axis=0), planes))
    row_other = from_partner(row_half)

    def in_order(value, other):
        low = jnp.where(core == 0, value, other)
        return jnp.stack([low, jnp.where(core == 0, other, value)])

    row_terms = in_order(row_half, row_other).reshape(rows, wide)
    own = rows // devices
    own_terms = lax.dynamic_slice_in_dim(row_terms, col * own, own, 0)
    terms = jnp.concatenate([disc[:, :slab].reshape(wide, width), disc[:, slab + depth * cut]], axis=0)
    other = from_partner(terms)
    col_terms = disc[:users, slab : slab + depth * cut].reshape(blocks, users // blocks, depth, cut, width)
    col_terms = col_terms.transpose(2, 1, 3, 0, 4).reshape(half, wide)
    updated, gains = closing(terms, other, row_terms, col_terms, own_terms, kron_inverse.T)
    return updated.T, gains.transpose(1, 0, 2)


def solution(mesh):
    return jax.shard_map(
        shards,
        mesh=mesh,
        in_specs=(P("row", "col"), P(None, None, "col")),
        out_specs=(P("row", "col"), P(None, ("row", "col"), None)),
        check_vma=False,
    )
```

```python
import functools

import jax
import jax.numpy as jnp
from jax import lax
from jax.experimental import pallas as pl
from jax.experimental.pallas import tpu as pltpu
from jax.sharding import PartitionSpec as P


highest = lax.Precision.HIGHEST
f32 = jnp.float32


def dot(a, b, dims=((1,), (0,))):
    return lax.dot_general(a, b, (dims, ((), ())), precision=highest, preferred_element_type=f32)


def rough(a, b):
    return jnp.dot(a.astype(jnp.bfloat16), b.astype(jnp.bfloat16), preferred_element_type=f32)


def unit(size):
    rows = lax.broadcasted_iota(jnp.int32, (size, size), 0)
    return (rows == lax.broadcasted_iota(jnp.int32, (size, size), 1)).astype(f32)


def expanded(block):
    eye = unit(block.shape[0])
    scale_col = lax.rsqrt(jnp.sum(block * eye, axis=1, keepdims=True))
    scale_row = lax.rsqrt(jnp.sum(block * eye, axis=0, keepdims=True))
    scaled = block * scale_col * scale_row
    off = scaled - eye
    square = rough(off, off)
    step = jnp.minimum(1.0, 1.9 / (1.0 + jnp.sqrt(jnp.sqrt(jnp.sum(square * square)))))
    rest = (1.0 - step) * eye - step * off
    guess = eye + rest
    rest = (1.0 - step) * (rest - step * off) + step * step * square
    for turn in range(2):
        more = rough(guess, rest)
        if turn < 1:
            rest = rough(rest, rest)
        guess = guess + more
    guess = guess * step
    rest = eye - dot(guess, scaled)
    miss = jnp.sum(rest * rest)
    guess = guess + rough(rest, guess)
    rest = eye - dot(guess, scaled)
    return (guess + rough(rest, guess)) * scale_col * scale_row, miss


def eliminated(block, work_ref):
    size = block.shape[0]
    lane = lax.broadcasted_iota(jnp.int32, (1, size), 1)
    line = lax.broadcasted_iota(jnp.int32, (size, 1), 0)
    work_ref[:size, :size] = block

    def sweep(at, carry):
        value = work_ref[:size, :size]
        row = jnp.sum(jnp.where(line == at, value, 0.0), axis=0, keepdims=True)
        here = lane == at
        col = jnp.sum(jnp.where(here, value, 0.0), axis=1, keepdims=True)
        pivot = 1.0 / jnp.sum(jnp.where(here, row, 0.0), axis=1, keepdims=True)
        row = jnp.where(here, pivot, row * pivot)
        col = jnp.where(line == at, 0.0, col)
        value = jnp.where(here, 0.0, value)
        work_ref[:size, :size] = jnp.where(line == at, row, value - col * row)
        return carry

    lax.fori_loop(0, size, sweep, 0)
    guess = work_ref[:size, :size]
    return guess + dot(unit(size) - dot(guess, block), guess)


def opening_kernel(core_ref, start_ref, lines_ref, keep_ref, send_ref):
    blocks, half, width = keep_ref.shape
    lines = jnp.concatenate([lines_ref[at] for at in range(blocks)], axis=1)
    value = dot(start_ref[...], lines, ((0,), (0,)))

    def store(low_ref, high_ref):
        for at in range(blocks):
            low_ref[at] = value[:half, at * width : (at + 1) * width]
            high_ref[at] = value[half:, at * width : (at + 1) * width]

    pl.when(core_ref[0] == 0)(lambda: store(keep_ref, send_ref))
    pl.when(core_ref[0] != 0)(lambda: store(send_ref, keep_ref))


def opening(core, start, lines):
    blocks, _, width = lines.shape
    in_vmem = pl.BlockSpec(memory_space=pltpu.VMEM)
    return pl.pallas_call(
        opening_kernel,
        out_shape=[pltpu.VMEM((blocks, start.shape[1] // 2, width), f32)] * 2,
        in_specs=[pl.BlockSpec(memory_space=pltpu.SMEM), in_vmem, in_vmem],
    )(core.reshape(1), start, lines)


def spread_kernel(got_ref, out_ref):
    piece = jnp.sum(got_ref[:, : out_ref.shape[1]], axis=0)
    for at in range(out_ref.shape[0]):
        out_ref[at] = piece


def spread(got, planes, held):
    return pl.pallas_call(
        spread_kernel,
        out_shape=pltpu.VMEM((planes, held, got.shape[2]), f32),
        in_specs=[pl.BlockSpec(memory_space=pltpu.VMEM)],
    )(pltpu.with_memory_space_constraint(got, pltpu.VMEM))


def slab_kernel(row_ref, got_ref, level_ref, send_ref, right_ref):
    depth, held, width = level_ref.shape
    share = held // 2
    tall = right_ref.shape[1]
    row = row_ref[0]
    slab = 2 * width // depth
    groups = width // slab
    packed = got_ref[:, held : held + tall // groups, :]
    packed = jnp.broadcast_to(packed[:, :, None, :], (depth, tall // groups, groups, width))
    packed = pltpu.roll(packed.reshape(depth * tall, width), slab, 1, stride=slab, stride_axis=0)
    right_ref[...] = jnp.zeros(right_ref.shape, f32)
    right_ref[:, :share, :width] = level_ref[:, :share, :]
    right_ref[:, :share, width:] = level_ref[:, share:, :]
    terms = dot(packed[:, :slab], right_ref[...].reshape(depth * tall, 2 * width), ((0,), (0,)))
    terms = pltpu.roll(terms, jnp.where(row == 0, 0, 2 * width - slab * row), 1)
    lane = lax.broadcasted_iota(jnp.int32, (slab, width), 1)
    block = jnp.where(lane < slab, terms[:, width:], 0.0)
    turned = jnp.concatenate([block, jnp.zeros((width - slab, width), f32)], axis=0).T
    block = jnp.where(row < depth // 2, block[: slab // 2], turned[slab // 2 : slab])
    block = jnp.concatenate([block[at : at + 1] for at in reversed(range(slab // 2))], axis=0)
    block = jnp.sum(pltpu.roll(block, 0, 1, stride=slab, stride_axis=0), axis=0, keepdims=True)
    piece = level_ref[row]
    cut = held // depth
    rest = held % depth
    part = level_ref[:, pl.ds(cut * row, cut), :]
    spare = level_ref[:, pl.ds(cut * depth + lax.rem(row, rest), 1), :]
    for at in range(depth):
        send_ref[at, :slab] = terms[:, :width]
        send_ref[at, slab : slab + held] = piece
        send_ref[at, slab + held : slab + held + cut] = part[at]
        send_ref[at, slab + held + cut : slab + held + cut + 1] = spare[at]
        send_ref[at, slab + held + cut + 1 :] = block


def slab_terms(row, got, level):
    depth, held, width = level.shape
    cut = held // depth
    slab = 2 * width // depth
    tall = -(-held // 2 // 8) * 8
    in_vmem = pl.BlockSpec(memory_space=pltpu.VMEM)
    return pl.pallas_call(
        slab_kernel,
        out_shape=pltpu.VMEM((depth, slab + held + cut + 2, width), f32),
        in_specs=[pl.BlockSpec(memory_space=pltpu.SMEM), in_vmem, in_vmem],
        scratch_shapes=[pltpu.VMEM((depth, tall, 2 * width), f32)],
    )(row.reshape(1), *(pltpu.with_memory_space_constraint(x, pltpu.VMEM) for x in (got, level)))


def plane_kernel(row_ref, line_ref, send_ref, *, slab):
    planes, rows, _ = send_ref.shape
    depth, tall, _ = line_ref.shape
    cut, turns = divmod(rows - slab - 1, depth)
    terms = jnp.sum(line_ref[:, :slab], axis=0)
    far = jnp.sum(line_ref[:, tall - 1 :], axis=0)
    spare = line_ref[pl.ds(row_ref[0] // (depth // turns) * turns, turns), tall - 2]
    for at in range(planes):
        send_ref[at, :slab] = terms
        for z in range(depth):
            first = slab + z * cut
            send_ref[at, first : first + cut] = line_ref[z, tall - 2 - cut : tall - 2]
        send_ref[at, rows - 1 - turns : rows - 1] = spare
        send_ref[at, rows - 1 :] = far


def plane_terms(row, line, rows, slab):
    planes = line.shape[0]
    return pl.pallas_call(
        functools.partial(plane_kernel, slab=slab),
        out_shape=jax.ShapeDtypeStruct((planes, rows, line.shape[2]), f32),
        in_specs=[pl.BlockSpec(memory_space=pltpu.SMEM), pl.BlockSpec(memory_space=pltpu.VMEM)],
    )(row.reshape(1), pltpu.with_memory_space_constraint(line, pltpu.VMEM))


def closing_kernel(mine_ref, other_ref, rows_ref, cols_ref, own_ref, start_ref, out_ref, gain_ref, work_ref):
    width = work_ref.shape[0] // 2
    slab = mine_ref.shape[0] - 2 * width
    groups = width // slab
    terms = mine_ref[...] + other_ref[...]

    far = [terms[2 * width + n + m : 2 * width + n + m + 1] for n in range(groups) for m in (0, groups)]
    far = jnp.concatenate([jnp.broadcast_to(part, (slab // 2, width)) for part in far], axis=0)
    far = pltpu.roll(far, slab, 1, stride=slab, stride_axis=0)

    def stepped(value):
        parts = [value[n * slab : (n + 1) * slab] for n in range(groups)]
        return jnp.concatenate([pltpu.roll(part, n * slab, 1) if n else part for n, part in enumerate(parts)], axis=0)

    across = lax.broadcasted_iota(jnp.int32, (width, width), 1) // slab
    down = lax.broadcasted_iota(jnp.int32, (width, width), 0) // slab
    upper, lower, far = stepped(terms[:width]), stepped(terms[width : 2 * width]), stepped(far)
    upper_turned, lower_turned = upper.T, lower.T
    cross = jnp.where(across < down, upper, jnp.where(across > down, lower_turned, far))
    upper = jnp.where(across >= down, upper, upper_turned) + unit(width)
    lower = jnp.where(across >= down, lower, lower_turned) + unit(width)

    top = jnp.concatenate([upper, cross], axis=1)
    system = jnp.concatenate([top, jnp.concatenate([cross.T, lower], axis=1)], axis=0)

    def solve(inverse):
        first, miss = inverse(upper)
        full, more = inverse(system)
        gain_ref[:, 0] = dot(own_ref[:, :width], first)
        gain_ref[:, 1] = dot(own_ref[...], full[:, width:])
        out_ref[...] = start_ref[...] - dot(dot(cols_ref[...], full), rows_ref[...], ((1,), (1,)))
        return miss + more

    miss = solve(expanded)

    @pl.when(jnp.logical_not(miss < 1e-2))
    def _():
        solve(lambda value: (eliminated(value, work_ref), 0.0))


def closing(*operands):
    own, start = operands[4:]
    width = own.shape[1] // 2
    in_vmem = pl.BlockSpec(memory_space=pltpu.VMEM)
    return pl.pallas_call(
        closing_kernel,
        out_shape=[
            jax.ShapeDtypeStruct(start.shape, f32),
            jax.ShapeDtypeStruct((own.shape[0], 2, width), f32),
        ],
        in_specs=[in_vmem] * len(operands),
        scratch_shapes=[pltpu.VMEM((2 * width, 2 * width), f32)],
    )(*(pltpu.with_memory_space_constraint(x, pltpu.VMEM) for x in operands))


def shards(kron_inverse, activations):
    rows, cols = kron_inverse.shape
    blocks, width = activations.shape[:2]
    wide = blocks * width
    planes = lax.axis_size("row")
    devices = lax.axis_size("col")
    depth = devices // 2
    row = lax.axis_index("row")
    col = lax.axis_index("col")
    lines = [[2 * z + k for z in range(depth)] for k in range(2)]

    def from_partner(value):
        return lax.ppermute(value, "col", [(at, at ^ 1) for at in range(devices)])

    def over_z(value):
        return lax.all_to_all(value, "col", 0, 0, tiled=True, axis_index_groups=lines)

    def over_plane(value):
        return lax.all_to_all(value, "row", 0, 0, tiled=True)

    half = rows // 2
    share = half // depth
    slab = wide // planes

    def whole(value):
        left = value[:, :share].reshape(half, width)
        return jnp.concatenate([left, value[:, share:].reshape(half, width)], axis=1)

    core = col % 2
    turned = activations.transpose(0, 2, 1)
    keep, send = opening(core, kron_inverse.T, turned)
    summed = keep + from_partner(send)
    groups = width // slab
    mine = lax.dynamic_slice(turned, (row // groups, 0, row % groups * slab), (1, cols, slab))
    mine = jnp.pad(mine.reshape(depth, share, slab), ((0, 0), (0, -share % groups), (0, 0)))
    mine = jnp.flip(mine.reshape(depth, -1, groups, slab), 2).reshape(depth, -1, width)
    parts = [summed[at].reshape(depth, share, width) for at in range(blocks)]
    got = over_z(jnp.concatenate([*parts, mine], axis=1))
    held = blocks * share
    level = over_plane(spread(got, planes, held))
    cut = held // planes
    rest = held % planes
    turns = depth // rest
    line = over_z(slab_terms(row, got, level))
    row_half = whole(line[:, slab : slab + held])
    disc = over_plane(plane_terms(row, line, slab + depth * cut + turns + 1, slab))
    row_other = from_partner(row_half)

    def in_order(value, other):
        low = jnp.where(core == 0, value, other)
        return jnp.stack([low, jnp.where(core == 0, other, value)])

    row_terms = in_order(row_half, row_other).reshape(rows, wide)
    own = rows // devices
    own_terms = lax.dynamic_slice_in_dim(row_terms, col * own, own, 0)
    terms = jnp.concatenate([disc[:, :slab].reshape(wide, width), disc[:, -1]], axis=0)
    other = from_partner(terms)
    part = disc[:, slab : slab + depth * cut].reshape(planes, depth, cut, width)
    part = part.transpose(1, 0, 2, 3).reshape(depth, planes * cut, width)
    spare = disc[:, slab + depth * cut : -1].reshape(-1, rest, turns, width)
    spare = spare.transpose(0, 2, 1, 3).reshape(depth, rest, width)
    col_terms = whole(jnp.concatenate([part, spare], axis=1))
    updated, gains = closing(terms, other, row_terms, col_terms, own_terms, kron_inverse.T)
    return updated.T, gains.transpose(1, 0, 2)


def solution(mesh):
    return jax.shard_map(
        shards,
        mesh=mesh,
        in_specs=(P("row", "col"), P(None, None, "col")),
        out_specs=(P("row", "col"), P(None, ("row", "col"), None)),
        check_vma=False,
    )
```

```python
import functools

import jax
import jax.numpy as jnp
from jax import lax
from jax.experimental import pallas as pl
from jax.experimental.pallas import tpu as pltpu
from jax.sharding import PartitionSpec as P

highest = lax.Precision.HIGHEST
f32 = jnp.float32


def dot(a, b, dims=((1,), (0,))):
    return lax.dot_general(a, b, (dims, ((), ())), precision=highest, preferred_element_type=f32)


def rough(a, b):
    return jnp.dot(a.astype(jnp.bfloat16), b.astype(jnp.bfloat16), preferred_element_type=f32)


def unit(size):
    rows = lax.broadcasted_iota(jnp.int32, (size, size), 0)
    return (rows == lax.broadcasted_iota(jnp.int32, (size, size), 1)).astype(f32)


def expanded(block):
    eye = unit(block.shape[0])
    scale_col = lax.rsqrt(jnp.sum(block * eye, axis=1, keepdims=True))
    scale_row = lax.rsqrt(jnp.sum(block * eye, axis=0, keepdims=True))
    scaled = block * scale_col * scale_row
    off = scaled - eye
    square = rough(off, off)
    step = jnp.minimum(1.0, 1.9 / (1.0 + jnp.sqrt(jnp.sqrt(jnp.sum(square * square)))))
    rest = (1.0 - step) * eye - step * off
    guess = eye + rest
    rest = (1.0 - step) * (rest - step * off) + step * step * square
    for turn in range(2):
        more = rough(guess, rest)
        if turn < 1:
            rest = rough(rest, rest)
        guess = guess + more
    guess = guess * step
    rest = eye - dot(guess, scaled)
    miss = jnp.sum(rest * rest)
    guess = guess + rough(rest, guess)
    rest = eye - dot(guess, scaled)
    return (guess + rough(rest, guess)) * scale_col * scale_row, miss


def eliminated(block, work_ref):
    size = block.shape[0]
    lane = lax.broadcasted_iota(jnp.int32, (1, size), 1)
    line = lax.broadcasted_iota(jnp.int32, (size, 1), 0)
    work_ref[:size, :size] = block

    def sweep(at, carry):
        value = work_ref[:size, :size]
        row = jnp.sum(jnp.where(line == at, value, 0.0), axis=0, keepdims=True)
        here = lane == at
        col = jnp.sum(jnp.where(here, value, 0.0), axis=1, keepdims=True)
        pivot = 1.0 / jnp.sum(jnp.where(here, row, 0.0), axis=1, keepdims=True)
        row = jnp.where(here, pivot, row * pivot)
        col = jnp.where(line == at, 0.0, col)
        value = jnp.where(here, 0.0, value)
        work_ref[:size, :size] = jnp.where(line == at, row, value - col * row)
        return carry

    lax.fori_loop(0, size, sweep, 0)
    guess = work_ref[:size, :size]
    return guess + dot(unit(size) - dot(guess, block), guess)


def opening_kernel(col_ref, start_ref, lines_ref, keep_ref, send_ref):
    blocks, half, width = keep_ref.shape
    lines = jnp.concatenate([lines_ref[at] for at in range(blocks)], axis=1)
    value = dot(start_ref[...], lines, ((0,), (0,)))

    def store(low_ref, high_ref):
        for at in range(blocks):
            low_ref[at] = value[:half, at * width : (at + 1) * width]
            high_ref[at] = value[half:, at * width : (at + 1) * width]

    pl.when(lax.rem(col_ref[0], 2) == 0)(lambda: store(keep_ref, send_ref))
    pl.when(lax.rem(col_ref[0], 2) != 0)(lambda: store(send_ref, keep_ref))


def opening(col, start, lines):
    blocks, _, width = lines.shape
    in_vmem = pl.BlockSpec(memory_space=pltpu.VMEM)
    return pl.pallas_call(
        opening_kernel,
        out_shape=[pltpu.VMEM((blocks, start.shape[1] // 2, width), f32)] * 2,
        in_specs=[pl.BlockSpec(memory_space=pltpu.SMEM), in_vmem, in_vmem],
    )(col.reshape(1), start, lines)


def spread_kernel(got_ref, out_ref):
    piece = jnp.sum(got_ref[:, : out_ref.shape[1]], axis=0)
    for at in range(out_ref.shape[0]):
        out_ref[at] = piece


def spread(got, planes, held):
    return pl.pallas_call(
        spread_kernel,
        out_shape=pltpu.VMEM((planes, held, got.shape[2]), f32),
        in_specs=[pl.BlockSpec(memory_space=pltpu.VMEM)],
    )(pltpu.with_memory_space_constraint(got, pltpu.VMEM))


def slab_kernel(row_ref, got_ref, level_ref, send_ref, right_ref):
    depth, held, width = level_ref.shape
    share = held // 2
    tall = right_ref.shape[1]
    row = row_ref[0]
    slab = 2 * width // depth
    groups = width // slab
    packed = got_ref[:, held : held + tall // groups, :]
    packed = jnp.broadcast_to(packed[:, :, None, :], (depth, tall // groups, groups, width))
    packed = pltpu.roll(packed.reshape(depth * tall, width), slab, 1, stride=slab, stride_axis=0)
    right_ref[...] = jnp.zeros(right_ref.shape, f32)
    right_ref[:, :share, :width] = level_ref[:, :share, :]
    right_ref[:, :share, width:] = level_ref[:, share:, :]
    terms = dot(packed[:, :slab], right_ref[...].reshape(depth * tall, 2 * width), ((0,), (0,)))
    terms = pltpu.roll(terms, jnp.where(row == 0, 0, 2 * width - slab * row), 1)
    lane = lax.broadcasted_iota(jnp.int32, (slab, width), 1)
    block = jnp.where(lane < slab, terms[:, width:], 0.0)
    turned = jnp.concatenate([block, jnp.zeros((width - slab, width), f32)], axis=0).T
    block = jnp.where(row < depth // 2, block[: slab // 2], turned[slab // 2 : slab])
    block = jnp.concatenate([block[at : at + 1] for at in reversed(range(slab // 2))], axis=0)
    block = jnp.sum(pltpu.roll(block, 0, 1, stride=slab, stride_axis=0), axis=0, keepdims=True)
    piece = level_ref[row]
    cut = held // depth
    rest = held % depth
    part = level_ref[:, pl.ds(cut * row, cut), :]
    spare = level_ref[:, pl.ds(cut * depth + lax.rem(row, rest), 1), :]
    for at in range(depth):
        send_ref[at, :slab] = terms[:, :width]
        send_ref[at, slab : slab + held] = piece
        send_ref[at, slab + held : slab + held + cut] = part[at]
        send_ref[at, slab + held + cut : slab + held + cut + 1] = spare[at]
        send_ref[at, slab + held + cut + 1 :] = block


def slab_terms(row, got, level):
    depth, held, width = level.shape
    cut = held // depth
    slab = 2 * width // depth
    tall = -(-held // 2 // 8) * 8
    in_vmem = pl.BlockSpec(memory_space=pltpu.VMEM)
    return pl.pallas_call(
        slab_kernel,
        out_shape=pltpu.VMEM((depth, slab + held + cut + 2, width), f32),
        in_specs=[pl.BlockSpec(memory_space=pltpu.SMEM), in_vmem, in_vmem],
        scratch_shapes=[pltpu.VMEM((depth, tall, 2 * width), f32)],
    )(row.reshape(1), *(pltpu.with_memory_space_constraint(x, pltpu.VMEM) for x in (got, level)))


def plane_kernel(row_ref, line_ref, send_ref, rows_ref, *, slab):
    planes, rows, _ = send_ref.shape
    depth, tall, width = line_ref.shape
    cut, turns = divmod(rows - slab - 1, depth)
    terms = jnp.sum(line_ref[:, :slab], axis=0)
    far = jnp.sum(line_ref[:, tall - 1 :], axis=0)
    spare = line_ref[pl.ds(row_ref[0] // (depth // turns) * turns, turns), tall - 2]
    half = rows_ref.shape[0] // 2
    share = half // depth
    for z in range(depth):
        rows_ref[z * share : (z + 1) * share] = line_ref[z, slab : slab + share]
        rows_ref[half + z * share : half + (z + 1) * share] = line_ref[z, slab + share : slab + 2 * share]
    for at in range(planes):
        send_ref[at, :slab] = terms
        for z in range(depth):
            first = slab + z * cut
            send_ref[at, first : first + cut] = line_ref[z, tall - 2 - cut : tall - 2]
        send_ref[at, rows - 1 - turns : rows - 1] = spare
        send_ref[at, rows - 1 :] = far


def plane_terms(row, line, rows, slab, held):
    planes, _, width = line.shape
    return pl.pallas_call(
        functools.partial(plane_kernel, slab=slab),
        out_shape=[pltpu.VMEM((planes, rows, width), f32), pltpu.VMEM((planes * held, width), f32)],
        in_specs=[pl.BlockSpec(memory_space=pltpu.SMEM), pl.BlockSpec(memory_space=pltpu.VMEM)],
    )(row.reshape(1), pltpu.with_memory_space_constraint(line, pltpu.VMEM))


def closing_kernel(col_ref, mine_ref, other_ref, cols_ref, start_ref, out_ref, gain_ref, work_ref, left_ref, right_ref):
    width = work_ref.shape[0] // 2
    half = left_ref.shape[0] // 2
    small = mine_ref.shape[0] - 2 * half
    slab = small - 2 * width
    groups = width // slab
    terms = mine_ref[:small] + other_ref[:small]

    def place(low, high):
        for at, part_ref in ((0, low), (half, high)):
            left_ref[at : at + half] = part_ref[small : small + half]
            right_ref[at : at + half] = part_ref[small + half :]

    pl.when(lax.rem(col_ref[0], 2) == 0)(lambda: place(mine_ref, other_ref))
    pl.when(lax.rem(col_ref[0], 2) != 0)(lambda: place(other_ref, mine_ref))
    own = pl.ds(col_ref[0] * gain_ref.shape[0], gain_ref.shape[0])

    far = [terms[2 * width + n + m : 2 * width + n + m + 1] for n in range(groups) for m in (0, groups)]
    far = jnp.concatenate([jnp.broadcast_to(part, (slab // 2, width)) for part in far], axis=0)
    far = pltpu.roll(far, slab, 1, stride=slab, stride_axis=0)

    def stepped(value):
        parts = [value[n * slab : (n + 1) * slab] for n in range(groups)]
        return jnp.concatenate([pltpu.roll(part, n * slab, 1) if n else part for n, part in enumerate(parts)], axis=0)

    across = lax.broadcasted_iota(jnp.int32, (width, width), 1) // slab
    down = lax.broadcasted_iota(jnp.int32, (width, width), 0) // slab
    upper, lower, far = stepped(terms[:width]), stepped(terms[width : 2 * width]), stepped(far)
    upper_turned, lower_turned = upper.T, lower.T
    cross = jnp.where(across < down, upper, jnp.where(across > down, lower_turned, far))
    upper = jnp.where(across >= down, upper, upper_turned) + unit(width)
    lower = jnp.where(across >= down, lower, lower_turned) + unit(width)

    top = jnp.concatenate([upper, cross], axis=1)
    system = jnp.concatenate([top, jnp.concatenate([cross.T, lower], axis=1)], axis=0)

    def solve(inverse):
        first, miss = inverse(upper)
        full, more = inverse(system)
        gain_ref[:, 0] = dot(left_ref[own], first)
        gain_ref[:, 1] = dot(jnp.concatenate([left_ref[own], right_ref[own]], axis=1), full[:, width:])
        rows = jnp.concatenate([left_ref[...], right_ref[...]], axis=1)
        out_ref[...] = start_ref[...] - dot(dot(cols_ref[...], full), rows, ((1,), (1,)))
        return miss + more

    miss = solve(expanded)

    @pl.when(jnp.logical_not(miss < 1e-2))
    def _():
        solve(lambda value: (eliminated(value, work_ref), 0.0))


def closing(col, terms, other, col_terms, start, own):
    cols, rows = start.shape
    width = terms.shape[1]
    in_vmem = pl.BlockSpec(memory_space=pltpu.VMEM)
    return pl.pallas_call(
        closing_kernel,
        out_shape=[jax.ShapeDtypeStruct(start.shape, f32), jax.ShapeDtypeStruct((own, 2, width), f32)],
        in_specs=[pl.BlockSpec(memory_space=pltpu.SMEM)] + [in_vmem] * 4,
        scratch_shapes=[pltpu.VMEM((2 * width, 2 * width), f32)] + [pltpu.VMEM((rows, width), f32)] * 2,
    )(col.reshape(1), *(pltpu.with_memory_space_constraint(x, pltpu.VMEM) for x in (terms, other, col_terms, start)))


def shards(kron_inverse, activations):
    rows, cols = kron_inverse.shape
    blocks, width = activations.shape[:2]
    wide = blocks * width
    planes = lax.axis_size("row")
    devices = lax.axis_size("col")
    depth = devices // 2
    row = lax.axis_index("row")
    col = lax.axis_index("col")
    lines = [[2 * z + k for z in range(depth)] for k in range(2)]

    def from_partner(value):
        return lax.ppermute(value, "col", [(at, at ^ 1) for at in range(devices)])

    def over_z(value):
        return lax.all_to_all(value, "col", 0, 0, tiled=True, axis_index_groups=lines)

    def over_plane(value):
        return lax.all_to_all(value, "row", 0, 0, tiled=True)

    half = rows // 2
    share = half // depth
    slab = wide // planes

    def whole(value):
        left = value[:, :share].reshape(half, width)
        return jnp.concatenate([left, value[:, share:].reshape(half, width)], axis=1)

    turned = activations.transpose(0, 2, 1)
    keep, send = opening(col, kron_inverse.T, turned)
    summed = keep + from_partner(send)
    groups = width // slab
    mine = lax.dynamic_slice(turned, (row // groups, 0, row % groups * slab), (1, cols, slab))
    mine = jnp.pad(mine.reshape(depth, share, slab), ((0, 0), (0, -share % groups), (0, 0)))
    mine = jnp.flip(mine.reshape(depth, -1, groups, slab), 2).reshape(depth, -1, width)
    parts = [summed[at].reshape(depth, share, width) for at in range(blocks)]
    got = over_z(jnp.concatenate([*parts, mine], axis=1))
    held = blocks * share
    level = over_plane(spread(got, planes, held))
    cut = held // planes
    rest = held % planes
    turns = depth // rest
    line = over_z(slab_terms(row, got, level))
    send, row_half = plane_terms(row, line, slab + depth * cut + turns + 1, slab, held)
    disc = over_plane(send)
    terms = jnp.concatenate([disc[:, :slab].reshape(wide, width), disc[:, -1], row_half], axis=0)
    other = from_partner(terms)
    part = disc[:, slab : slab + depth * cut].reshape(planes, depth, cut, width)
    part = part.transpose(1, 0, 2, 3).reshape(depth, planes * cut, width)
    spare = disc[:, slab + depth * cut : -1].reshape(-1, rest, turns, width)
    spare = spare.transpose(0, 2, 1, 3).reshape(depth, rest, width)
    col_terms = whole(jnp.concatenate([part, spare], axis=1))
    updated, gains = closing(col, terms, other, col_terms, kron_inverse.T, rows // devices)
    return updated.T, gains.transpose(1, 0, 2)


def solution(mesh):
    return jax.shard_map(
        shards,
        mesh=mesh,
        in_specs=(P("row", "col"), P(None, None, "col")),
        out_specs=(P("row", "col"), P(None, ("row", "col"), None)),
        check_vma=False,
    )
```

```python
import functools

import jax
import jax.numpy as jnp
from jax import lax
from jax.experimental import pallas as pl
from jax.experimental.pallas import tpu as pltpu
from jax.sharding import PartitionSpec as P

highest = lax.Precision.HIGHEST
f32 = jnp.float32


def dot(a, b, dims=((1,), (0,))):
    return lax.dot_general(a, b, (dims, ((), ())), precision=highest, preferred_element_type=f32)


def rough(a, b):
    return jnp.dot(a.astype(jnp.bfloat16), b.astype(jnp.bfloat16), preferred_element_type=f32)


def unit(size):
    rows = lax.broadcasted_iota(jnp.int32, (size, size), 0)
    return (rows == lax.broadcasted_iota(jnp.int32, (size, size), 1)).astype(f32)


def expanded(block):
    eye = unit(block.shape[0])
    scale_col = lax.rsqrt(jnp.sum(block * eye, axis=1, keepdims=True))
    scale_row = lax.rsqrt(jnp.sum(block * eye, axis=0, keepdims=True))
    scaled = block * scale_col * scale_row
    off = scaled - eye
    square = rough(off, off)
    step = jnp.minimum(1.0, 1.9 / (1.0 + jnp.sqrt(jnp.sqrt(jnp.sum(square * square)))))
    rest = (1.0 - step) * eye - step * off
    guess = eye + rest
    rest = (1.0 - step) * (rest - step * off) + step * step * square
    for turn in range(2):
        more = rough(guess, rest)
        if turn < 1:
            rest = rough(rest, rest)
        guess = guess + more
    guess = guess * step
    rest = eye - dot(guess, scaled)
    miss = jnp.sum(rest * rest)
    guess = guess + rough(rest, guess)
    rest = eye - dot(guess, scaled)
    return (guess + rough(rest, guess)) * scale_col * scale_row, miss


def eliminated(block, work_ref):
    size = block.shape[0]
    lane = lax.broadcasted_iota(jnp.int32, (1, size), 1)
    line = lax.broadcasted_iota(jnp.int32, (size, 1), 0)
    work_ref[:size, :size] = block

    def sweep(at, carry):
        value = work_ref[:size, :size]
        row = jnp.sum(jnp.where(line == at, value, 0.0), axis=0, keepdims=True)
        here = lane == at
        col = jnp.sum(jnp.where(here, value, 0.0), axis=1, keepdims=True)
        pivot = 1.0 / jnp.sum(jnp.where(here, row, 0.0), axis=1, keepdims=True)
        row = jnp.where(here, pivot, row * pivot)
        col = jnp.where(line == at, 0.0, col)
        value = jnp.where(here, 0.0, value)
        work_ref[:size, :size] = jnp.where(line == at, row, value - col * row)
        return carry

    lax.fori_loop(0, size, sweep, 0)
    guess = work_ref[:size, :size]
    return guess + dot(unit(size) - dot(guess, block), guess)


def product(high, start_ref, lines_ref, out_ref):
    blocks, half, width = out_ref.shape
    lines = jnp.concatenate([lines_ref[at] for at in range(blocks)], axis=1)

    def store(first):
        value = dot(start_ref[:, first : first + half], lines, ((0,), (0,)))
        for at in range(blocks):
            out_ref[at] = value[:, at * width : (at + 1) * width]

    pl.when(high == 0)(lambda: store(0))
    pl.when(high != 0)(lambda: store(half))


def loading_kernel(col_ref, far_start_ref, far_lines_ref, send_ref, start_ref, lines_ref, done_ref):
    moves = (
        pltpu.make_async_copy(far_start_ref, start_ref, done_ref.at[0]),
        pltpu.make_async_copy(far_lines_ref, lines_ref, done_ref.at[1]),
    )
    for move in moves:
        move.start()
    for move in moves:
        move.wait()
    product(1 - lax.rem(col_ref[0], 2), start_ref, lines_ref, send_ref)


def loading(col, start, lines):
    blocks, _, width = lines.shape
    in_hbm = pl.BlockSpec(memory_space=pl.ANY)
    return pl.pallas_call(
        loading_kernel,
        out_shape=[
            pltpu.VMEM((blocks, start.shape[1] // 2, width), f32),
            pltpu.VMEM(start.shape, f32),
            pltpu.VMEM(lines.shape, f32),
        ],
        in_specs=[pl.BlockSpec(memory_space=pltpu.SMEM), in_hbm, in_hbm],
        scratch_shapes=[pltpu.SemaphoreType.DMA((2,))],
    )(col.reshape(1), start, lines)


def keeping_kernel(col_ref, start_ref, lines_ref, out_ref):
    product(lax.rem(col_ref[0], 2), start_ref, lines_ref, out_ref)


def keeping(col, start, lines):
    blocks, _, width = lines.shape
    in_vmem = pl.BlockSpec(memory_space=pltpu.VMEM)
    return pl.pallas_call(
        keeping_kernel,
        out_shape=pltpu.VMEM((blocks, start.shape[1] // 2, width), f32),
        in_specs=[pl.BlockSpec(memory_space=pltpu.SMEM), in_vmem, in_vmem],
    )(col.reshape(1), *(pltpu.with_memory_space_constraint(x, pltpu.VMEM) for x in (start, lines)))


def spread_kernel(got_ref, out_ref):
    piece = jnp.sum(got_ref[:, : out_ref.shape[1]], axis=0)
    for at in range(out_ref.shape[0]):
        out_ref[at] = piece


def spread(got, planes, held):
    return pl.pallas_call(
        spread_kernel,
        out_shape=pltpu.VMEM((planes, held, got.shape[2]), f32),
        in_specs=[pl.BlockSpec(memory_space=pltpu.VMEM)],
    )(pltpu.with_memory_space_constraint(got, pltpu.VMEM))


def slab_kernel(row_ref, got_ref, level_ref, send_ref, right_ref):
    depth, held, width = level_ref.shape
    share = held // 2
    tall = right_ref.shape[1]
    row = row_ref[0]
    slab = 2 * width // depth
    groups = width // slab
    packed = got_ref[:, held : held + tall // groups, :]
    packed = jnp.broadcast_to(packed[:, :, None, :], (depth, tall // groups, groups, width))
    packed = pltpu.roll(packed.reshape(depth * tall, width), slab, 1, stride=slab, stride_axis=0)
    right_ref[...] = jnp.zeros(right_ref.shape, f32)
    right_ref[:, :share, :width] = level_ref[:, :share, :]
    right_ref[:, :share, width:] = level_ref[:, share:, :]
    terms = dot(packed[:, :slab], right_ref[...].reshape(depth * tall, 2 * width), ((0,), (0,)))
    terms = pltpu.roll(terms, jnp.where(row == 0, 0, 2 * width - slab * row), 1)
    lane = lax.broadcasted_iota(jnp.int32, (slab, width), 1)
    block = jnp.where(lane < slab, terms[:, width:], 0.0)
    turned = jnp.concatenate([block, jnp.zeros((width - slab, width), f32)], axis=0).T
    block = jnp.where(row < depth // 2, block[: slab // 2], turned[slab // 2 : slab])
    block = jnp.concatenate([block[at : at + 1] for at in reversed(range(slab // 2))], axis=0)
    block = jnp.sum(pltpu.roll(block, 0, 1, stride=slab, stride_axis=0), axis=0, keepdims=True)
    piece = level_ref[row]
    cut = held // depth
    rest = held % depth
    part = level_ref[:, pl.ds(cut * row, cut), :]
    spare = level_ref[:, pl.ds(cut * depth + lax.rem(row, rest), 1), :]
    for at in range(depth):
        send_ref[at, :slab] = terms[:, :width]
        send_ref[at, slab : slab + held] = piece
        send_ref[at, slab + held : slab + held + cut] = part[at]
        send_ref[at, slab + held + cut : slab + held + cut + 1] = spare[at]
        send_ref[at, slab + held + cut + 1 :] = block


def slab_terms(row, got, level):
    depth, held, width = level.shape
    cut = held // depth
    slab = 2 * width // depth
    tall = -(-held // 2 // 8) * 8
    in_vmem = pl.BlockSpec(memory_space=pltpu.VMEM)
    return pl.pallas_call(
        slab_kernel,
        out_shape=pltpu.VMEM((depth, slab + held + cut + 2, width), f32),
        in_specs=[pl.BlockSpec(memory_space=pltpu.SMEM), in_vmem, in_vmem],
        scratch_shapes=[pltpu.VMEM((depth, tall, 2 * width), f32)],
    )(row.reshape(1), *(pltpu.with_memory_space_constraint(x, pltpu.VMEM) for x in (got, level)))


def plane_kernel(row_ref, line_ref, send_ref, rows_ref, *, slab):
    planes, rows, _ = send_ref.shape
    depth, tall, width = line_ref.shape
    cut, turns = divmod(rows - slab - 1, depth)
    terms = jnp.sum(line_ref[:, :slab], axis=0)
    far = jnp.sum(line_ref[:, tall - 1 :], axis=0)
    spare = line_ref[pl.ds(row_ref[0] // (depth // turns) * turns, turns), tall - 2]
    half = rows_ref.shape[0] // 2
    share = half // depth
    for z in range(depth):
        rows_ref[z * share : (z + 1) * share] = line_ref[z, slab : slab + share]
        rows_ref[half + z * share : half + (z + 1) * share] = line_ref[z, slab + share : slab + 2 * share]
    for at in range(planes):
        send_ref[at, :slab] = terms
        for z in range(depth):
            first = slab + z * cut
            send_ref[at, first : first + cut] = line_ref[z, tall - 2 - cut : tall - 2]
        send_ref[at, rows - 1 - turns : rows - 1] = spare
        send_ref[at, rows - 1 :] = far


def plane_terms(row, line, rows, slab, held):
    planes, _, width = line.shape
    return pl.pallas_call(
        functools.partial(plane_kernel, slab=slab),
        out_shape=[pltpu.VMEM((planes, rows, width), f32), pltpu.VMEM((planes * held, width), f32)],
        in_specs=[pl.BlockSpec(memory_space=pltpu.SMEM), pl.BlockSpec(memory_space=pltpu.VMEM)],
    )(row.reshape(1), pltpu.with_memory_space_constraint(line, pltpu.VMEM))


def closing_kernel(col_ref, mine_ref, other_ref, cols_ref, start_ref, out_ref, gain_ref, work_ref, left_ref, right_ref):
    width = work_ref.shape[0] // 2
    half = left_ref.shape[0] // 2
    small = mine_ref.shape[0] - 2 * half
    slab = small - 2 * width
    groups = width // slab
    terms = mine_ref[:small] + other_ref[:small]

    core = lax.rem(col_ref[0], 2)
    for at, part_ref in ((core, mine_ref), (1 - core, other_ref)):
        at = pl.ds(pl.multiple_of(at * half, 8), half)
        left_ref[at] = part_ref[small : small + half]
        right_ref[at] = part_ref[small + half :]
    own = pl.ds(col_ref[0] * gain_ref.shape[0], gain_ref.shape[0])

    far = [terms[2 * width + n + m : 2 * width + n + m + 1] for n in range(groups) for m in (0, groups)]
    far = jnp.concatenate([jnp.broadcast_to(part, (slab // 2, width)) for part in far], axis=0)
    far = pltpu.roll(far, slab, 1, stride=slab, stride_axis=0)

    def stepped(value):
        parts = [value[n * slab : (n + 1) * slab] for n in range(groups)]
        return jnp.concatenate([pltpu.roll(part, n * slab, 1) if n else part for n, part in enumerate(parts)], axis=0)

    across = lax.broadcasted_iota(jnp.int32, (width, width), 1) // slab
    down = lax.broadcasted_iota(jnp.int32, (width, width), 0) // slab
    upper, lower, far = stepped(terms[:width]), stepped(terms[width : 2 * width]), stepped(far)
    upper_turned, lower_turned = upper.T, lower.T
    cross = jnp.where(across < down, upper, jnp.where(across > down, lower_turned, far))
    upper = jnp.where(across >= down, upper, upper_turned) + unit(width)
    lower = jnp.where(across >= down, lower, lower_turned) + unit(width)

    top = jnp.concatenate([upper, cross], axis=1)
    system = jnp.concatenate([top, jnp.concatenate([cross.T, lower], axis=1)], axis=0)

    def solve(inverse):
        first, miss = inverse(upper)
        full, more = inverse(system)
        gain_ref[:, 0] = dot(left_ref[own], first)
        gain_ref[:, 1] = dot(jnp.concatenate([left_ref[own], right_ref[own]], axis=1), full[:, width:])
        rows = jnp.concatenate([left_ref[...], right_ref[...]], axis=1)
        out_ref[...] = start_ref[...] - dot(dot(cols_ref[...], full), rows, ((1,), (1,)))
        return miss + more

    miss = solve(expanded)

    @pl.when(jnp.logical_not(miss < 1e-2))
    def _():
        solve(lambda value: (eliminated(value, work_ref), 0.0))


def closing(col, terms, other, col_terms, start, own):
    cols, rows = start.shape
    width = terms.shape[1]
    in_vmem = pl.BlockSpec(memory_space=pltpu.VMEM)
    return pl.pallas_call(
        closing_kernel,
        out_shape=[jax.ShapeDtypeStruct(start.shape, f32), jax.ShapeDtypeStruct((own, 2, width), f32)],
        in_specs=[pl.BlockSpec(memory_space=pltpu.SMEM)] + [in_vmem] * 4,
        scratch_shapes=[pltpu.VMEM((2 * width, 2 * width), f32)] + [pltpu.VMEM((rows, width), f32)] * 2,
    )(col.reshape(1), *(pltpu.with_memory_space_constraint(x, pltpu.VMEM) for x in (terms, other, col_terms, start)))


def shards(kron_inverse, activations):
    rows, cols = kron_inverse.shape
    blocks, width = activations.shape[:2]
    wide = blocks * width
    planes = lax.axis_size("row")
    devices = lax.axis_size("col")
    depth = devices // 2
    row = lax.axis_index("row")
    col = lax.axis_index("col")
    lines = [[2 * z + k for z in range(depth)] for k in range(2)]

    def from_partner(value):
        return lax.ppermute(value, "col", [(at, at ^ 1) for at in range(devices)])

    def over_z(value):
        return lax.all_to_all(value, "col", 0, 0, tiled=True, axis_index_groups=lines)

    def over_plane(value):
        return lax.all_to_all(value, "row", 0, 0, tiled=True)

    half = rows // 2
    share = half // depth
    slab = wide // planes

    def whole(value):
        left = value[:, :share].reshape(half, width)
        return jnp.concatenate([left, value[:, share:].reshape(half, width)], axis=1)

    send, start, turned = loading(col, kron_inverse.T, activations.transpose(0, 2, 1))
    summed = keeping(col, start, turned) + from_partner(send)
    groups = width // slab
    mine = lax.dynamic_slice(turned, (row // groups, 0, row % groups * slab), (1, cols, slab))
    mine = jnp.pad(mine.reshape(depth, share, slab), ((0, 0), (0, -share % groups), (0, 0)))
    mine = jnp.flip(mine.reshape(depth, -1, groups, slab), 2).reshape(depth, -1, width)
    parts = [summed[at].reshape(depth, share, width) for at in range(blocks)]
    got = over_z(jnp.concatenate([*parts, mine], axis=1))
    held = blocks * share
    level = over_plane(spread(got, planes, held))
    cut = held // planes
    rest = held % planes
    turns = depth // rest
    line = over_z(slab_terms(row, got, level))
    send, row_half = plane_terms(row, line, slab + depth * cut + turns + 1, slab, held)
    disc = over_plane(send)
    terms = jnp.concatenate([disc[:, :slab].reshape(wide, width), disc[:, -1], row_half], axis=0)
    other = from_partner(terms)
    part = disc[:, slab : slab + depth * cut].reshape(planes, depth, cut, width)
    part = part.transpose(1, 0, 2, 3).reshape(depth, planes * cut, width)
    spare = disc[:, slab + depth * cut : -1].reshape(-1, rest, turns, width)
    spare = spare.transpose(0, 2, 1, 3).reshape(depth, rest, width)
    col_terms = whole(jnp.concatenate([part, spare], axis=1))
    updated, gains = closing(col, terms, other, col_terms, start, rows // devices)
    return updated.T, gains.transpose(1, 0, 2)


def solution(mesh):
    return jax.shard_map(
        shards,
        mesh=mesh,
        in_specs=(P("row", "col"), P(None, None, "col")),
        out_specs=(P("row", "col"), P(None, ("row", "col"), None)),
        check_vma=False,
    )
```

```python
import functools

import jax
import jax.numpy as jnp
from jax import lax
from jax.experimental import pallas as pl
from jax.experimental.pallas import tpu as pltpu
from jax.sharding import PartitionSpec as P

highest = lax.Precision.HIGHEST
f32 = jnp.float32


def dot(a, b, dims=((1,), (0,))):
    return lax.dot_general(a, b, (dims, ((), ())), precision=highest, preferred_element_type=f32)


def rough(a, b):
    return jnp.dot(a.astype(jnp.bfloat16), b.astype(jnp.bfloat16), preferred_element_type=f32)


def unit(size):
    rows = lax.broadcasted_iota(jnp.int32, (size, size), 0)
    return (rows == lax.broadcasted_iota(jnp.int32, (size, size), 1)).astype(f32)


def expanded(block):
    eye = unit(block.shape[0])
    scale_col = lax.rsqrt(jnp.sum(block * eye, axis=1, keepdims=True))
    scale_row = lax.rsqrt(jnp.sum(block * eye, axis=0, keepdims=True))
    scaled = block * scale_col * scale_row
    off = scaled - eye
    square = rough(off, off)
    spread = jnp.sum(jnp.sum(square * square, axis=0, keepdims=True), axis=1, keepdims=True)
    step = jnp.minimum(1.0, 1.9 / (1.0 + jnp.sqrt(jnp.sqrt(spread))))
    rest = (1.0 - step) * eye - step * off
    guess = eye + rest
    rest = (1.0 - step) * (rest - step * off) + step * step * square
    for turn in range(2):
        more = rough(guess, rest)
        if turn < 1:
            rest = rough(rest, rest)
        guess = guess + more
    guess = guess * step
    rest = eye - dot(guess, scaled)
    miss = jnp.sum(rest * rest)
    guess = guess + rough(rest, guess)
    rest = eye - dot(guess, scaled)
    return (guess + rough(rest, guess)) * scale_col * scale_row, miss


def eliminated(block, work_ref):
    size = block.shape[0]
    lane = lax.broadcasted_iota(jnp.int32, (1, size), 1)
    line = lax.broadcasted_iota(jnp.int32, (size, 1), 0)
    work_ref[:size, :size] = block

    def sweep(at, carry):
        value = work_ref[:size, :size]
        row = jnp.sum(jnp.where(line == at, value, 0.0), axis=0, keepdims=True)
        here = lane == at
        col = jnp.sum(jnp.where(here, value, 0.0), axis=1, keepdims=True)
        pivot = 1.0 / jnp.sum(jnp.where(here, row, 0.0), axis=1, keepdims=True)
        row = jnp.where(here, pivot, row * pivot)
        col = jnp.where(line == at, 0.0, col)
        value = jnp.where(here, 0.0, value)
        work_ref[:size, :size] = jnp.where(line == at, row, value - col * row)
        return carry

    lax.fori_loop(0, size, sweep, 0)
    guess = work_ref[:size, :size]
    return guess + dot(unit(size) - dot(guess, block), guess)


def product(high, start_ref, lines_ref, out_ref):
    blocks, half, width = out_ref.shape
    lines = jnp.concatenate([lines_ref[at] for at in range(blocks)], axis=1)

    def store(first):
        value = dot(start_ref[:, first : first + half], lines, ((0,), (0,)))
        for at in range(blocks):
            out_ref[at] = value[:, at * width : (at + 1) * width]

    pl.when(high == 0)(lambda: store(0))
    pl.when(high != 0)(lambda: store(half))


def loading_kernel(col_ref, far_start_ref, far_lines_ref, send_ref, start_ref, lines_ref, done_ref):
    moves = (
        pltpu.make_async_copy(far_start_ref, start_ref, done_ref.at[0]),
        pltpu.make_async_copy(far_lines_ref, lines_ref, done_ref.at[1]),
    )
    for move in moves:
        move.start()
    for move in moves:
        move.wait()
    product(1 - lax.rem(col_ref[0], 2), start_ref, lines_ref, send_ref)


def loading(col, start, lines):
    blocks, _, width = lines.shape
    in_hbm = pl.BlockSpec(memory_space=pl.ANY)
    return pl.pallas_call(
        loading_kernel,
        out_shape=[
            pltpu.VMEM((blocks, start.shape[1] // 2, width), f32),
            pltpu.VMEM(start.shape, f32),
            pltpu.VMEM(lines.shape, f32),
        ],
        in_specs=[pl.BlockSpec(memory_space=pltpu.SMEM), in_hbm, in_hbm],
        scratch_shapes=[pltpu.SemaphoreType.DMA((2,))],
    )(col.reshape(1), start, lines)


def keeping_kernel(col_ref, start_ref, lines_ref, out_ref):
    product(lax.rem(col_ref[0], 2), start_ref, lines_ref, out_ref)


def keeping(col, start, lines):
    blocks, _, width = lines.shape
    in_vmem = pl.BlockSpec(memory_space=pltpu.VMEM)
    return pl.pallas_call(
        keeping_kernel,
        out_shape=pltpu.VMEM((blocks, start.shape[1] // 2, width), f32),
        in_specs=[pl.BlockSpec(memory_space=pltpu.SMEM), in_vmem, in_vmem],
    )(col.reshape(1), *(pltpu.with_memory_space_constraint(x, pltpu.VMEM) for x in (start, lines)))


def spread_kernel(got_ref, out_ref):
    piece = jnp.sum(got_ref[:, : out_ref.shape[1]], axis=0)
    for at in range(out_ref.shape[0]):
        out_ref[at] = piece


def spread(got, planes, held):
    return pl.pallas_call(
        spread_kernel,
        out_shape=pltpu.VMEM((planes, held, got.shape[2]), f32),
        in_specs=[pl.BlockSpec(memory_space=pltpu.VMEM)],
    )(pltpu.with_memory_space_constraint(got, pltpu.VMEM))


def slab_kernel(row_ref, got_ref, level_ref, send_ref, right_ref, *, seats):
    depth, held, width = level_ref.shape
    share = held // 2
    tall = right_ref.shape[1]
    row = row_ref[0]
    slab = 2 * width // depth
    groups = width // slab
    packed = got_ref[:, held : held + tall // groups, :]
    packed = jnp.broadcast_to(packed[:, :, None, :], (depth, tall // groups, groups, width))
    packed = pltpu.roll(packed.reshape(depth * tall, width), slab, 1, stride=slab, stride_axis=0)
    right_ref[...] = jnp.zeros(right_ref.shape, f32)
    for at, seat in enumerate(seats):
        right_ref[at, :share, :width] = level_ref[seat, :share, :]
        right_ref[at, :share, width:] = level_ref[seat, share:, :]
    terms = dot(packed[:, :slab], right_ref[...].reshape(depth * tall, 2 * width), ((0,), (0,)))
    terms = pltpu.roll(terms, jnp.where(row == 0, 0, 2 * width - slab * row), 1)
    lane = lax.broadcasted_iota(jnp.int32, (slab, width), 1)
    block = jnp.where(lane < slab, terms[:, width:], 0.0)
    turned = jnp.concatenate([block, jnp.zeros((width - slab, width), f32)], axis=0).T
    block = jnp.where(row < depth // 2, block[: slab // 2], turned[slab // 2 : slab])
    block = jnp.concatenate([block[at : at + 1] for at in reversed(range(slab // 2))], axis=0)
    block = jnp.sum(pltpu.roll(block, 0, 1, stride=slab, stride_axis=0), axis=0, keepdims=True)
    piece = level_ref[row]
    cut = held // depth
    rest = held % depth
    part = level_ref[:, pl.ds(cut * row, cut), :]
    spare = level_ref[:, pl.ds(cut * depth + lax.rem(row, rest), 1), :]
    for at, seat in enumerate(seats):
        send_ref[at, :slab] = terms[:, :width]
        send_ref[at, slab : slab + held] = piece
        send_ref[at, slab + held : slab + held + cut] = part[seat]
        send_ref[at, slab + held + cut : slab + held + cut + 1] = spare[seat]
        send_ref[at, slab + held + cut + 1 :] = block


def slab_terms(row, got, level, seats):
    depth, held, width = level.shape
    cut = held // depth
    slab = 2 * width // depth
    tall = -(-held // 2 // 8) * 8
    in_vmem = pl.BlockSpec(memory_space=pltpu.VMEM)
    return pl.pallas_call(
        functools.partial(slab_kernel, seats=seats),
        out_shape=pltpu.VMEM((depth, slab + held + cut + 2, width), f32),
        in_specs=[pl.BlockSpec(memory_space=pltpu.SMEM), in_vmem, in_vmem],
        scratch_shapes=[pltpu.VMEM((depth, tall, 2 * width), f32)],
    )(row.reshape(1), *(pltpu.with_memory_space_constraint(x, pltpu.VMEM) for x in (got, level)))


def plane_kernel(row_ref, line_ref, send_ref, rows_ref, *, slab):
    planes, rows, _ = send_ref.shape
    depth, tall, width = line_ref.shape
    cut, turns = divmod(rows - slab - 1, depth)
    terms = jnp.sum(line_ref[:, :slab], axis=0)
    far = jnp.sum(line_ref[:, tall - 1 :], axis=0)
    spare = line_ref[pl.ds(row_ref[0] // (depth // turns) * turns, turns), tall - 2]
    half = rows_ref.shape[0] // 2
    share = half // depth
    for z in range(depth):
        rows_ref[z * share : (z + 1) * share] = line_ref[z, slab : slab + share]
        rows_ref[half + z * share : half + (z + 1) * share] = line_ref[z, slab + share : slab + 2 * share]
    for at in range(planes):
        send_ref[at, :slab] = terms
        for z in range(depth):
            first = slab + z * cut
            send_ref[at, first : first + cut] = line_ref[z, tall - 2 - cut : tall - 2]
        send_ref[at, rows - 1 - turns : rows - 1] = spare
        send_ref[at, rows - 1 :] = far


def plane_terms(row, line, rows, slab, held):
    planes, _, width = line.shape
    return pl.pallas_call(
        functools.partial(plane_kernel, slab=slab),
        out_shape=[pltpu.VMEM((planes, rows, width), f32), pltpu.VMEM((planes * held, width), f32)],
        in_specs=[pl.BlockSpec(memory_space=pltpu.SMEM), pl.BlockSpec(memory_space=pltpu.VMEM)],
    )(row.reshape(1), pltpu.with_memory_space_constraint(line, pltpu.VMEM))


def closing_kernel(col_ref, mine_ref, other_ref, cols_ref, start_ref, out_ref, gain_ref, work_ref, left_ref, right_ref):
    width = work_ref.shape[0] // 2
    half = left_ref.shape[0] // 2
    small = mine_ref.shape[0] - 2 * half
    slab = small - 2 * width
    groups = width // slab
    terms = mine_ref[:small] + other_ref[:small]

    core = lax.rem(col_ref[0], 2)
    for at, part_ref in ((core, mine_ref), (1 - core, other_ref)):
        at = pl.ds(pl.multiple_of(at * half, 8), half)
        left_ref[at] = part_ref[small : small + half]
        right_ref[at] = part_ref[small + half :]
    own = pl.ds(col_ref[0] * gain_ref.shape[0], gain_ref.shape[0])

    far = [terms[2 * width + n + m : 2 * width + n + m + 1] for n in range(groups) for m in (0, groups)]
    far = jnp.concatenate([jnp.broadcast_to(part, (slab // 2, width)) for part in far], axis=0)
    far = pltpu.roll(far, slab, 1, stride=slab, stride_axis=0)

    def stepped(value):
        parts = [value[n * slab : (n + 1) * slab] for n in range(groups)]
        return jnp.concatenate([pltpu.roll(part, n * slab, 1) if n else part for n, part in enumerate(parts)], axis=0)

    across = lax.broadcasted_iota(jnp.int32, (width, width), 1) // slab
    down = lax.broadcasted_iota(jnp.int32, (width, width), 0) // slab
    upper, lower, far = stepped(terms[:width]), stepped(terms[width : 2 * width]), stepped(far)
    upper_turned, lower_turned = upper.T, lower.T
    cross = jnp.where(across < down, upper, jnp.where(across > down, lower_turned, far))
    upper = jnp.where(across >= down, upper, upper_turned) + unit(width)
    lower = jnp.where(across >= down, lower, lower_turned) + unit(width)

    top = jnp.concatenate([upper, cross], axis=1)
    system = jnp.concatenate([top, jnp.concatenate([cross.T, lower], axis=1)], axis=0)

    def solve(inverse):
        first, miss = inverse(upper)
        full, more = inverse(system)
        gain_ref[:, 0] = dot(left_ref[own], first)
        gain_ref[:, 1] = dot(jnp.concatenate([left_ref[own], right_ref[own]], axis=1), full[:, width:])
        rows = jnp.concatenate([left_ref[...], right_ref[...]], axis=1)
        out_ref[...] = start_ref[...] - dot(dot(cols_ref[...], full), rows, ((1,), (1,)))
        return miss + more

    miss = solve(expanded)

    @pl.when(jnp.logical_not(miss < 1e-2))
    def _():
        solve(lambda value: (eliminated(value, work_ref), 0.0))


def closing(col, terms, other, col_terms, start, own):
    cols, rows = start.shape
    width = terms.shape[1]
    in_vmem = pl.BlockSpec(memory_space=pltpu.VMEM)
    return pl.pallas_call(
        closing_kernel,
        out_shape=[jax.ShapeDtypeStruct(start.shape, f32), jax.ShapeDtypeStruct((own, 2, width), f32)],
        in_specs=[pl.BlockSpec(memory_space=pltpu.SMEM)] + [in_vmem] * 4,
        scratch_shapes=[pltpu.VMEM((2 * width, 2 * width), f32)] + [pltpu.VMEM((rows, width), f32)] * 2,
    )(col.reshape(1), *(pltpu.with_memory_space_constraint(x, pltpu.VMEM) for x in (terms, other, col_terms, start)))


def mirrored(count):
    order = [0]
    while len(order) < count:
        order = [2 * at for at in order] + [2 * at + 1 for at in order]
    return order


def shards(kron_inverse, activations):
    rows, cols = kron_inverse.shape
    blocks, width = activations.shape[:2]
    wide = blocks * width
    planes = lax.axis_size("row")
    devices = lax.axis_size("col")
    depth = devices // 2
    along = mirrored(depth)
    around = [seat // 2 + seat % 2 * (planes // 2) for seat in range(planes)]
    seats = [around.index(z) for z in along]
    row = lax.axis_index("row")
    row = row % (planes // 2) * 2 + row // (planes // 2)
    col = lax.axis_index("col")
    lines = [[2 * z + k for z in along] for k in range(2)]

    def from_partner(value):
        return lax.ppermute(value, "col", [(at, at ^ 1) for at in range(devices)])

    def over_z(value):
        return lax.all_to_all(value, "col", 0, 0, tiled=True, axis_index_groups=lines)

    def over_plane(value):
        return lax.all_to_all(value, "row", 0, 0, tiled=True, axis_index_groups=[around])

    half = rows // 2
    share = half // depth
    slab = wide // planes

    def whole(value):
        left = value[:, :share].reshape(half, width)
        return jnp.concatenate([left, value[:, share:].reshape(half, width)], axis=1)

    send, start, turned = loading(col, kron_inverse.T, activations.transpose(0, 2, 1))
    summed = keeping(col, start, turned) + from_partner(send)
    groups = width // slab
    mine = lax.dynamic_slice(turned, (row // groups, 0, row % groups * slab), (1, cols, slab))
    mine = jnp.pad(mine.reshape(depth, share, slab), ((0, 0), (0, -share % groups), (0, 0)))
    mine = jnp.flip(mine.reshape(depth, -1, groups, slab), 2).reshape(depth, -1, width)
    parts = [summed[at].reshape(depth, share, width) for at in range(blocks)]
    got = over_z(jnp.concatenate([*parts, mine], axis=1))
    held = blocks * share
    level = over_plane(spread(got, planes, held))
    cut = held // planes
    rest = held % planes
    turns = depth // rest
    line = over_z(slab_terms(row, got, level, seats))
    send, row_half = plane_terms(row, line, slab + depth * cut + turns + 1, slab, held)
    disc = over_plane(send)
    terms = jnp.concatenate([disc[:, :slab].reshape(wide, width), disc[:, -1], row_half], axis=0)
    other = from_partner(terms)
    part = disc[:, slab : slab + depth * cut].reshape(planes, depth, cut, width)
    part = part.transpose(1, 0, 2, 3).reshape(depth, planes * cut, width)
    spare = disc[:, slab + depth * cut : -1].reshape(-1, rest, turns, width)
    spare = spare.transpose(0, 2, 1, 3).reshape(depth, rest, width)
    col_terms = whole(jnp.concatenate([part, spare], axis=1))
    updated, gains = closing(col, terms, other, col_terms, start, rows // devices)
    return updated.T, gains.transpose(1, 0, 2)


def solution(mesh):
    return jax.shard_map(
        shards,
        mesh=mesh,
        in_specs=(P("row", "col"), P(None, None, "col")),
        out_specs=(P("row", "col"), P(None, ("row", "col"), None)),
        check_vma=False,
    )
```

```python
import functools

import jax
import jax.numpy as jnp
from jax import lax
from jax.experimental import pallas as pl
from jax.experimental.pallas import tpu as pltpu
from jax.sharding import PartitionSpec as P

highest = lax.Precision.HIGHEST
f32 = jnp.float32


def dot(a, b, dims=((1,), (0,))):
    return lax.dot_general(a, b, (dims, ((), ())), precision=highest, preferred_element_type=f32)


def rough(a, b):
    return jnp.dot(a.astype(jnp.bfloat16), b.astype(jnp.bfloat16), preferred_element_type=f32)


def unit(size):
    rows = lax.broadcasted_iota(jnp.int32, (size, size), 0)
    return (rows == lax.broadcasted_iota(jnp.int32, (size, size), 1)).astype(f32)


def expanded(block):
    eye = unit(block.shape[0])
    scale_col = lax.rsqrt(jnp.sum(block * eye, axis=1, keepdims=True))
    scale_row = lax.rsqrt(jnp.sum(block * eye, axis=0, keepdims=True))
    scaled = block * scale_col * scale_row
    off = scaled - eye
    square = rough(off, off)
    spread = jnp.sum(jnp.sum(square * square, axis=0, keepdims=True), axis=1, keepdims=True)
    step = jnp.minimum(1.0, 1.9 / (1.0 + jnp.sqrt(jnp.sqrt(spread))))
    rest = (1.0 - step) * eye - step * off
    guess = eye + rest
    rest = (1.0 - step) * (rest - step * off) + step * step * square
    for turn in range(2):
        more = rough(guess, rest)
        if turn < 1:
            rest = rough(rest, rest)
        guess = guess + more
    guess = guess * step
    rest = eye - dot(guess, scaled)
    miss = jnp.sum(rest * rest)
    guess = guess + rough(rest, guess)
    rest = eye - dot(guess, scaled)
    return (guess + rough(rest, guess)) * scale_col * scale_row, miss


def eliminated(block, work_ref):
    size = block.shape[0]
    lane = lax.broadcasted_iota(jnp.int32, (1, size), 1)
    line = lax.broadcasted_iota(jnp.int32, (size, 1), 0)
    work_ref[:size, :size] = block

    def sweep(at, carry):
        value = work_ref[:size, :size]
        row = jnp.sum(jnp.where(line == at, value, 0.0), axis=0, keepdims=True)
        here = lane == at
        col = jnp.sum(jnp.where(here, value, 0.0), axis=1, keepdims=True)
        pivot = 1.0 / jnp.sum(jnp.where(here, row, 0.0), axis=1, keepdims=True)
        row = jnp.where(here, pivot, row * pivot)
        col = jnp.where(line == at, 0.0, col)
        value = jnp.where(here, 0.0, value)
        work_ref[:size, :size] = jnp.where(line == at, row, value - col * row)
        return carry

    lax.fori_loop(0, size, sweep, 0)
    guess = work_ref[:size, :size]
    return guess + dot(unit(size) - dot(guess, block), guess)


def product(high, start_ref, lines_ref, out_ref):
    blocks, half, width = out_ref.shape
    lines = jnp.concatenate([lines_ref[at] for at in range(blocks)], axis=1)

    def store(first):
        value = dot(start_ref[:, first : first + half], lines, ((0,), (0,)))
        for at in range(blocks):
            out_ref[at] = value[:, at * width : (at + 1) * width]

    pl.when(high == 0)(lambda: store(0))
    pl.when(high != 0)(lambda: store(half))


def loading_kernel(col_ref, far_start_ref, far_lines_ref, send_ref, start_ref, lines_ref, done_ref):
    moves = (
        pltpu.make_async_copy(far_start_ref, start_ref, done_ref.at[0]),
        pltpu.make_async_copy(far_lines_ref, lines_ref, done_ref.at[1]),
    )
    for move in moves:
        move.start()
    for move in moves:
        move.wait()
    product(1 - lax.rem(col_ref[0], 2), start_ref, lines_ref, send_ref)


def loading(col, start, lines):
    blocks, _, width = lines.shape
    in_hbm = pl.BlockSpec(memory_space=pl.ANY)
    return pl.pallas_call(
        loading_kernel,
        out_shape=[
            pltpu.VMEM((blocks, start.shape[1] // 2, width), f32),
            pltpu.VMEM(start.shape, f32),
            pltpu.VMEM(lines.shape, f32),
        ],
        in_specs=[pl.BlockSpec(memory_space=pltpu.SMEM), in_hbm, in_hbm],
        scratch_shapes=[pltpu.SemaphoreType.DMA((2,))],
    )(col.reshape(1), start, lines)


def keeping_kernel(col_ref, start_ref, lines_ref, out_ref):
    product(lax.rem(col_ref[0], 2), start_ref, lines_ref, out_ref)


def keeping(col, start, lines):
    blocks, _, width = lines.shape
    in_vmem = pl.BlockSpec(memory_space=pltpu.VMEM)
    return pl.pallas_call(
        keeping_kernel,
        out_shape=pltpu.VMEM((blocks, start.shape[1] // 2, width), f32),
        in_specs=[pl.BlockSpec(memory_space=pltpu.SMEM), in_vmem, in_vmem],
    )(col.reshape(1), *(pltpu.with_memory_space_constraint(x, pltpu.VMEM) for x in (start, lines)))


def spread_kernel(got_ref, out_ref):
    piece = jnp.sum(got_ref[:, : out_ref.shape[1]], axis=0)
    for at in range(out_ref.shape[0]):
        out_ref[at] = piece


def spread(got, planes, held):
    return pl.pallas_call(
        spread_kernel,
        out_shape=pltpu.VMEM((planes, held, got.shape[2]), f32),
        in_specs=[pl.BlockSpec(memory_space=pltpu.VMEM)],
    )(pltpu.with_memory_space_constraint(got, pltpu.VMEM))


def slab_kernel(row_ref, got_ref, level_ref, send_ref, right_ref, *, seats):
    depth, held, width = level_ref.shape
    share = held // 2
    tall = right_ref.shape[1]
    row = row_ref[0]
    slab = 2 * width // depth
    groups = width // slab
    packed = got_ref[:, held : held + tall // groups, :]
    packed = jnp.broadcast_to(packed[:, :, None, :], (depth, tall // groups, groups, width))
    packed = pltpu.roll(packed.reshape(depth * tall, width), slab, 1, stride=slab, stride_axis=0)
    right_ref[...] = jnp.zeros(right_ref.shape, f32)
    for at, seat in enumerate(seats):
        right_ref[at, :share, :width] = level_ref[seat, :share, :]
        right_ref[at, :share, width:] = level_ref[seat, share:, :]
    terms = dot(packed[:, :slab], right_ref[...].reshape(depth * tall, 2 * width), ((0,), (0,)))
    terms = pltpu.roll(terms, jnp.where(row == 0, 0, 2 * width - slab * row), 1)
    lane = lax.broadcasted_iota(jnp.int32, (slab, width), 1)
    block = jnp.where(lane < slab, terms[:, width:], 0.0)
    turned = jnp.concatenate([block, jnp.zeros((width - slab, width), f32)], axis=0).T
    block = jnp.where(row < depth // 2, block[: slab // 2], turned[slab // 2 : slab])
    block = jnp.concatenate([block[at : at + 1] for at in reversed(range(slab // 2))], axis=0)
    block = jnp.sum(pltpu.roll(block, 0, 1, stride=slab, stride_axis=0), axis=0, keepdims=True)
    piece = level_ref[row]
    cut = held // depth
    rest = held % depth
    part = level_ref[:, pl.ds(cut * row, cut), :]
    spare = level_ref[:, pl.ds(cut * depth + lax.rem(row, rest), 1), :]
    for at, seat in enumerate(seats):
        send_ref[at, :slab] = terms[:, :width]
        send_ref[at, slab : slab + held] = piece
        send_ref[at, slab + held : slab + held + cut] = part[seat]
        send_ref[at, slab + held + cut : slab + held + cut + 1] = spare[seat]
        send_ref[at, slab + held + cut + 1 :] = block


def slab_terms(row, got, level, seats):
    depth, held, width = level.shape
    cut = held // depth
    slab = 2 * width // depth
    tall = -(-held // 2 // 8) * 8
    in_vmem = pl.BlockSpec(memory_space=pltpu.VMEM)
    return pl.pallas_call(
        functools.partial(slab_kernel, seats=seats),
        out_shape=pltpu.VMEM((depth, slab + held + cut + 2, width), f32),
        in_specs=[pl.BlockSpec(memory_space=pltpu.SMEM), in_vmem, in_vmem],
        scratch_shapes=[pltpu.VMEM((depth, tall, 2 * width), f32)],
    )(row.reshape(1), *(pltpu.with_memory_space_constraint(x, pltpu.VMEM) for x in (got, level)))


def plane_kernel(row_ref, line_ref, send_ref, rows_ref, *, slab):
    planes, rows, _ = send_ref.shape
    depth, tall, width = line_ref.shape
    cut, turns = divmod(rows - slab - 1, depth)
    terms = jnp.sum(line_ref[:, :slab], axis=0)
    far = jnp.sum(line_ref[:, tall - 1 :], axis=0)
    spare = line_ref[pl.ds(row_ref[0] // (depth // turns) * turns, turns), tall - 2]
    half = rows_ref.shape[0] // 2
    share = half // depth
    for z in range(depth):
        rows_ref[z * share : (z + 1) * share] = line_ref[z, slab : slab + share]
        rows_ref[half + z * share : half + (z + 1) * share] = line_ref[z, slab + share : slab + 2 * share]
    for at in range(planes):
        send_ref[at, :slab] = terms
        for z in range(depth):
            first = slab + z * cut
            send_ref[at, first : first + cut] = line_ref[z, tall - 2 - cut : tall - 2]
        send_ref[at, rows - 1 - turns : rows - 1] = spare
        send_ref[at, rows - 1 :] = far


def plane_terms(row, line, rows, slab, held):
    planes, _, width = line.shape
    return pl.pallas_call(
        functools.partial(plane_kernel, slab=slab),
        out_shape=[pltpu.VMEM((planes, rows, width), f32), pltpu.VMEM((planes * held, width), f32)],
        in_specs=[pl.BlockSpec(memory_space=pltpu.SMEM), pl.BlockSpec(memory_space=pltpu.VMEM)],
    )(row.reshape(1), pltpu.with_memory_space_constraint(line, pltpu.VMEM))


def closing_kernel(col_ref, mine_ref, other_ref, cols_ref, start_ref, out_ref, gain_ref, work_ref, left_ref, right_ref):
    width = work_ref.shape[0] // 2
    half = left_ref.shape[0] // 2
    small = mine_ref.shape[0] - 2 * half
    slab = small - 2 * width
    groups = width // slab
    terms = mine_ref[:small] + other_ref[:small]

    core = lax.rem(col_ref[0], 2)
    for at, part_ref in ((core, mine_ref), (1 - core, other_ref)):
        at = pl.ds(pl.multiple_of(at * half, 8), half)
        left_ref[at] = part_ref[small : small + half]
        right_ref[at] = part_ref[small + half :]
    own = pl.ds(col_ref[0] * gain_ref.shape[0], gain_ref.shape[0])

    far = [terms[2 * width + n + m : 2 * width + n + m + 1] for n in range(groups) for m in (0, groups)]
    far = jnp.concatenate([jnp.broadcast_to(part, (slab // 2, width)) for part in far], axis=0)
    far = pltpu.roll(far, slab, 1, stride=slab, stride_axis=0)

    def stepped(value):
        parts = [value[n * slab : (n + 1) * slab] for n in range(groups)]
        return jnp.concatenate([pltpu.roll(part, n * slab, 1) if n else part for n, part in enumerate(parts)], axis=0)

    across = lax.broadcasted_iota(jnp.int32, (width, width), 1) // slab
    down = lax.broadcasted_iota(jnp.int32, (width, width), 0) // slab
    upper, lower, far = stepped(terms[:width]), stepped(terms[width : 2 * width]), stepped(far)
    upper_turned, lower_turned = upper.T, lower.T
    cross = jnp.where(across < down, upper, jnp.where(across > down, lower_turned, far))
    upper = jnp.where(across >= down, upper, upper_turned) + unit(width)
    lower = jnp.where(across >= down, lower, lower_turned) + unit(width)

    top = jnp.concatenate([upper, cross], axis=1)
    system = jnp.concatenate([top, jnp.concatenate([cross.T, lower], axis=1)], axis=0)

    def solve(inverse):
        first, miss = inverse(upper)
        full, more = inverse(system)
        gain_ref[:, 0] = dot(left_ref[own], first)
        gain_ref[:, 1] = dot(jnp.concatenate([left_ref[own], right_ref[own]], axis=1), full[:, width:])
        rows = jnp.concatenate([left_ref[...], right_ref[...]], axis=1)
        out_ref[...] = start_ref[...] - dot(dot(cols_ref[...], full), rows, ((1,), (1,)))
        return miss + more

    miss = solve(expanded)

    @pl.when(jnp.logical_not(miss < 1e-2))
    def _():
        solve(lambda value: (eliminated(value, work_ref), 0.0))


def closing(col, terms, other, col_terms, start, own):
    cols, rows = start.shape
    width = terms.shape[1]
    in_vmem = pl.BlockSpec(memory_space=pltpu.VMEM)
    return pl.pallas_call(
        closing_kernel,
        out_shape=[jax.ShapeDtypeStruct(start.shape, f32), jax.ShapeDtypeStruct((own, 2, width), f32)],
        in_specs=[pl.BlockSpec(memory_space=pltpu.SMEM)] + [in_vmem] * 4,
        scratch_shapes=[pltpu.VMEM((2 * width, 2 * width), f32)] + [pltpu.VMEM((rows, width), f32)] * 2,
    )(col.reshape(1), *(pltpu.with_memory_space_constraint(x, pltpu.VMEM) for x in (terms, other, col_terms, start)))


def shards(kron_inverse, activations):
    rows, cols = kron_inverse.shape
    blocks, width = activations.shape[:2]
    wide = blocks * width
    planes = lax.axis_size("row")
    devices = lax.axis_size("col")
    depth = devices // 2
    along = sorted(range(depth), key=lambda z: min(z, depth - z))
    around = [seat // 2 + seat % 2 * (planes // 2) for seat in range(planes)]
    seats = [around.index(z) for z in along]
    row = lax.axis_index("row")
    row = row % (planes // 2) * 2 + row // (planes // 2)
    col = lax.axis_index("col")
    lines = [[2 * z + k for z in along] for k in range(2)]

    def from_partner(value):
        return lax.ppermute(value, "col", [(at, at ^ 1) for at in range(devices)])

    def over_z(value):
        return lax.all_to_all(value, "col", 0, 0, tiled=True, axis_index_groups=lines)

    def over_plane(value):
        return lax.all_to_all(value, "row", 0, 0, tiled=True, axis_index_groups=[around])

    half = rows // 2
    share = half // depth
    slab = wide // planes

    def whole(value):
        left = value[:, :share].reshape(half, width)
        return jnp.concatenate([left, value[:, share:].reshape(half, width)], axis=1)

    send, start, turned = loading(col, kron_inverse.T, activations.transpose(0, 2, 1))
    summed = keeping(col, start, turned) + from_partner(send)
    groups = width // slab
    mine = lax.dynamic_slice(turned, (row // groups, 0, row % groups * slab), (1, cols, slab))
    mine = jnp.pad(mine.reshape(depth, share, slab), ((0, 0), (0, -share % groups), (0, 0)))
    mine = jnp.flip(mine.reshape(depth, -1, groups, slab), 2).reshape(depth, -1, width)
    parts = [summed[at].reshape(depth, share, width) for at in range(blocks)]
    got = over_z(jnp.concatenate([*parts, mine], axis=1))
    held = blocks * share
    level = over_plane(spread(got, planes, held))
    cut = held // planes
    rest = held % planes
    turns = depth // rest
    line = over_z(slab_terms(row, got, level, seats))
    send, row_half = plane_terms(row, line, slab + depth * cut + turns + 1, slab, held)
    disc = over_plane(send)
    terms = jnp.concatenate([disc[:, :slab].reshape(wide, width), disc[:, -1], row_half], axis=0)
    other = from_partner(terms)
    part = disc[:, slab : slab + depth * cut].reshape(planes, depth, cut, width)
    part = part.transpose(1, 0, 2, 3).reshape(depth, planes * cut, width)
    spare = disc[:, slab + depth * cut : -1].reshape(-1, rest, turns, width)
    spare = spare.transpose(0, 2, 1, 3).reshape(depth, rest, width)
    col_terms = whole(jnp.concatenate([part, spare], axis=1))
    updated, gains = closing(col, terms, other, col_terms, start, rows // devices)
    return updated.T, gains.transpose(1, 0, 2)


def solution(mesh):
    return jax.shard_map(
        shards,
        mesh=mesh,
        in_specs=(P("row", "col"), P(None, None, "col")),
        out_specs=(P("row", "col"), P(None, ("row", "col"), None)),
        check_vma=False,
    )
```

```python
import functools

import jax
import jax.numpy as jnp
from jax import lax
from jax.experimental import pallas as pl
from jax.experimental.pallas import tpu as pltpu
from jax.sharding import PartitionSpec as P

highest = lax.Precision.HIGHEST
f32 = jnp.float32


def dot(a, b, dims=((1,), (0,))):
    return lax.dot_general(a, b, (dims, ((), ())), precision=highest, preferred_element_type=f32)


def rough(a, b):
    return jnp.dot(a.astype(jnp.bfloat16), b.astype(jnp.bfloat16), preferred_element_type=f32)


def unit(size):
    rows = lax.broadcasted_iota(jnp.int32, (size, size), 0)
    return (rows == lax.broadcasted_iota(jnp.int32, (size, size), 1)).astype(f32)


def expanded(block):
    eye = unit(block.shape[0])
    scale_col = lax.rsqrt(jnp.sum(block * eye, axis=1, keepdims=True))
    scale_row = lax.rsqrt(jnp.sum(block * eye, axis=0, keepdims=True))
    scaled = block * scale_col * scale_row
    off = scaled - eye
    square = rough(off, off)
    spread = jnp.sum(jnp.sum(square * square, axis=0, keepdims=True), axis=1, keepdims=True)
    step = jnp.minimum(1.0, 1.9 / (1.0 + jnp.sqrt(jnp.sqrt(spread))))
    rest = (1.0 - step) * eye - step * off
    guess = eye + rest
    rest = (1.0 - step) * (rest - step * off) + step * step * square
    for turn in range(2):
        more = rough(guess, rest)
        if turn < 1:
            rest = rough(rest, rest)
        guess = guess + more
    guess = guess * step
    rest = eye - dot(guess, scaled)
    miss = jnp.sum(rest * rest)
    guess = guess + rough(rest, guess)
    rest = eye - dot(guess, scaled)
    return (guess + rough(rest, guess)) * scale_col * scale_row, miss


def eliminated(block, work_ref):
    size = block.shape[0]
    lane = lax.broadcasted_iota(jnp.int32, (1, size), 1)
    line = lax.broadcasted_iota(jnp.int32, (size, 1), 0)
    work_ref[:size, :size] = block

    def sweep(at, carry):
        value = work_ref[:size, :size]
        row = jnp.sum(jnp.where(line == at, value, 0.0), axis=0, keepdims=True)
        here = lane == at
        col = jnp.sum(jnp.where(here, value, 0.0), axis=1, keepdims=True)
        pivot = 1.0 / jnp.sum(jnp.where(here, row, 0.0), axis=1, keepdims=True)
        row = jnp.where(here, pivot, row * pivot)
        col = jnp.where(line == at, 0.0, col)
        value = jnp.where(here, 0.0, value)
        work_ref[:size, :size] = jnp.where(line == at, row, value - col * row)
        return carry

    lax.fori_loop(0, size, sweep, 0)
    guess = work_ref[:size, :size]
    return guess + dot(unit(size) - dot(guess, block), guess)


def product(high, start_ref, lines_ref, out_ref):
    blocks, half, width = out_ref.shape
    lines = jnp.concatenate([lines_ref[at] for at in range(blocks)], axis=1)

    def store(first):
        value = dot(start_ref[:, first : first + half], lines, ((0,), (0,)))
        for at in range(blocks):
            out_ref[at] = value[:, at * width : (at + 1) * width]

    pl.when(high == 0)(lambda: store(0))
    pl.when(high != 0)(lambda: store(half))


def loading_kernel(col_ref, far_start_ref, far_lines_ref, send_ref, start_ref, lines_ref, done_ref):
    moves = (
        pltpu.make_async_copy(far_start_ref, start_ref, done_ref.at[0]),
        pltpu.make_async_copy(far_lines_ref, lines_ref, done_ref.at[1]),
    )
    for move in moves:
        move.start()
    for move in moves:
        move.wait()
    product(1 - lax.rem(col_ref[0], 2), start_ref, lines_ref, send_ref)


def loading(col, start, lines):
    blocks, _, width = lines.shape
    in_hbm = pl.BlockSpec(memory_space=pl.ANY)
    return pl.pallas_call(
        loading_kernel,
        out_shape=[
            pltpu.VMEM((blocks, start.shape[1] // 2, width), f32),
            pltpu.VMEM(start.shape, f32),
            pltpu.VMEM(lines.shape, f32),
        ],
        in_specs=[pl.BlockSpec(memory_space=pltpu.SMEM), in_hbm, in_hbm],
        scratch_shapes=[pltpu.SemaphoreType.DMA((2,))],
    )(col.reshape(1), start, lines)


def keeping_kernel(col_ref, start_ref, lines_ref, out_ref):
    product(lax.rem(col_ref[0], 2), start_ref, lines_ref, out_ref)


def keeping(col, start, lines):
    blocks, _, width = lines.shape
    in_vmem = pl.BlockSpec(memory_space=pltpu.VMEM)
    return pl.pallas_call(
        keeping_kernel,
        out_shape=pltpu.VMEM((blocks, start.shape[1] // 2, width), f32),
        in_specs=[pl.BlockSpec(memory_space=pltpu.SMEM), in_vmem, in_vmem],
    )(col.reshape(1), *(pltpu.with_memory_space_constraint(x, pltpu.VMEM) for x in (start, lines)))


def spread_kernel(got_ref, out_ref):
    piece = jnp.sum(got_ref[:, : out_ref.shape[1]], axis=0)
    for at in range(out_ref.shape[0]):
        out_ref[at] = piece


def spread(got, planes, held):
    return pl.pallas_call(
        spread_kernel,
        out_shape=pltpu.VMEM((planes, held, got.shape[2]), f32),
        in_specs=[pl.BlockSpec(memory_space=pltpu.VMEM)],
    )(pltpu.with_memory_space_constraint(got, pltpu.VMEM))


def slab_kernel(row_ref, got_ref, level_ref, send_ref, right_ref, *, seats):
    depth, held, width = level_ref.shape
    share = held // 2
    tall = right_ref.shape[1]
    row = row_ref[0]
    slab = 2 * width // depth
    groups = width // slab
    packed = got_ref[:, held : held + tall // groups, :]
    packed = jnp.broadcast_to(packed[:, :, None, :], (depth, tall // groups, groups, width))
    packed = pltpu.roll(packed.reshape(depth * tall, width), slab, 1, stride=slab, stride_axis=0)
    right_ref[...] = jnp.zeros(right_ref.shape, f32)
    for at, seat in enumerate(seats):
        right_ref[at, :share, :width] = level_ref[seat, :share, :]
        right_ref[at, :share, width:] = level_ref[seat, share:, :]
    terms = dot(packed[:, :slab], right_ref[...].reshape(depth * tall, 2 * width), ((0,), (0,)))
    terms = pltpu.roll(terms, jnp.where(row == 0, 0, 2 * width - slab * row), 1)
    lane = lax.broadcasted_iota(jnp.int32, (slab, width), 1)
    block = jnp.where(lane < slab, terms[:, width:], 0.0)
    turned = jnp.concatenate([block, jnp.zeros((width - slab, width), f32)], axis=0).T
    block = jnp.where(row < depth // 2, block[: slab // 2], turned[slab // 2 : slab])
    block = jnp.concatenate([block[at : at + 1] for at in reversed(range(slab // 2))], axis=0)
    block = jnp.sum(pltpu.roll(block, 0, 1, stride=slab, stride_axis=0), axis=0, keepdims=True)
    piece = level_ref[row]
    cut = held // depth
    rest = held % depth
    part = level_ref[:, pl.ds(cut * row, cut), :]
    spare = level_ref[:, pl.ds(cut * depth + lax.rem(row, rest), 1), :]
    for at, seat in enumerate(seats):
        send_ref[at, :slab] = terms[:, :width]
        send_ref[at, slab : slab + held] = piece
        send_ref[at, slab + held : slab + held + cut] = part[seat]
        send_ref[at, slab + held + cut : slab + held + cut + 1] = spare[seat]
        send_ref[at, slab + held + cut + 1 :] = block


def slab_terms(row, got, level, seats):
    depth, held, width = level.shape
    cut = held // depth
    slab = 2 * width // depth
    tall = -(-held // 2 // 8) * 8
    in_vmem = pl.BlockSpec(memory_space=pltpu.VMEM)
    return pl.pallas_call(
        functools.partial(slab_kernel, seats=seats),
        out_shape=pltpu.VMEM((depth, slab + held + cut + 2, width), f32),
        in_specs=[pl.BlockSpec(memory_space=pltpu.SMEM), in_vmem, in_vmem],
        scratch_shapes=[pltpu.VMEM((depth, tall, 2 * width), f32)],
    )(row.reshape(1), *(pltpu.with_memory_space_constraint(x, pltpu.VMEM) for x in (got, level)))


def plane_kernel(row_ref, line_ref, send_ref, rows_ref, *, slab):
    planes, rows, _ = send_ref.shape
    depth, tall, width = line_ref.shape
    cut, turns = divmod(rows - slab - 1, depth)
    terms = jnp.sum(line_ref[:, :slab], axis=0)
    far = jnp.sum(line_ref[:, tall - 1 :], axis=0)
    spare = line_ref[pl.ds(row_ref[0] // (depth // turns) * turns, turns), tall - 2]
    half = rows_ref.shape[0] // 2
    share = half // depth
    for z in range(depth):
        rows_ref[z * share : (z + 1) * share] = line_ref[z, slab : slab + share]
        rows_ref[half + z * share : half + (z + 1) * share] = line_ref[z, slab + share : slab + 2 * share]
    for at in range(planes):
        send_ref[at, :slab] = terms
        for z in range(depth):
            first = slab + z * cut
            send_ref[at, first : first + cut] = line_ref[z, tall - 2 - cut : tall - 2]
        send_ref[at, rows - 1 - turns : rows - 1] = spare
        send_ref[at, rows - 1 :] = far


def plane_terms(row, line, rows, slab, held):
    planes, _, width = line.shape
    return pl.pallas_call(
        functools.partial(plane_kernel, slab=slab),
        out_shape=[pltpu.VMEM((planes, rows, width), f32), pltpu.VMEM((planes * held, width), f32)],
        in_specs=[pl.BlockSpec(memory_space=pltpu.SMEM), pl.BlockSpec(memory_space=pltpu.VMEM)],
    )(row.reshape(1), pltpu.with_memory_space_constraint(line, pltpu.VMEM))


def closing_kernel(col_ref, mine_ref, other_ref, cols_ref, start_ref, out_ref, gain_ref, work_ref, left_ref, right_ref):
    width = work_ref.shape[0] // 2
    half = left_ref.shape[0] // 2
    small = mine_ref.shape[0] - 2 * half
    slab = small - 2 * width
    groups = width // slab
    terms = mine_ref[:small] + other_ref[:small]

    core = lax.rem(col_ref[0], 2)
    for at, part_ref in ((core, mine_ref), (1 - core, other_ref)):
        at = pl.ds(pl.multiple_of(at * half, 8), half)
        left_ref[at] = part_ref[small : small + half]
        right_ref[at] = part_ref[small + half :]
    own = pl.ds(col_ref[0] * gain_ref.shape[0], gain_ref.shape[0])

    far = [terms[2 * width + n + m : 2 * width + n + m + 1] for n in range(groups) for m in (0, groups)]
    far = jnp.concatenate([jnp.broadcast_to(part, (slab // 2, width)) for part in far], axis=0)
    far = pltpu.roll(far, slab, 1, stride=slab, stride_axis=0)

    def stepped(value):
        parts = [value[n * slab : (n + 1) * slab] for n in range(groups)]
        return jnp.concatenate([pltpu.roll(part, n * slab, 1) if n else part for n, part in enumerate(parts)], axis=0)

    across = lax.broadcasted_iota(jnp.int32, (width, width), 1) // slab
    down = lax.broadcasted_iota(jnp.int32, (width, width), 0) // slab
    upper, lower, far = stepped(terms[:width]), stepped(terms[width : 2 * width]), stepped(far)
    upper_turned, lower_turned = upper.T, lower.T
    cross = jnp.where(across < down, upper, jnp.where(across > down, lower_turned, far))
    upper = jnp.where(across >= down, upper, upper_turned) + unit(width)
    lower = jnp.where(across >= down, lower, lower_turned) + unit(width)

    top = jnp.concatenate([upper, cross], axis=1)
    system = jnp.concatenate([top, jnp.concatenate([cross.T, lower], axis=1)], axis=0)

    def solve(inverse):
        first, miss = inverse(upper)
        full, more = inverse(system)
        gain_ref[:, 0] = dot(left_ref[own], first)
        gain_ref[:, 1] = dot(jnp.concatenate([left_ref[own], right_ref[own]], axis=1), full[:, width:])
        rows = jnp.concatenate([left_ref[...], right_ref[...]], axis=1)
        out_ref[...] = start_ref[...] - dot(dot(cols_ref[...], full), rows, ((1,), (1,)))
        return miss + more

    miss = solve(expanded)

    @pl.when(jnp.logical_not(miss < 1e-2))
    def _():
        solve(lambda value: (eliminated(value, work_ref), 0.0))


def closing(col, terms, other, col_terms, start, own):
    cols, rows = start.shape
    width = terms.shape[1]
    in_vmem = pl.BlockSpec(memory_space=pltpu.VMEM)
    return pl.pallas_call(
        closing_kernel,
        out_shape=[jax.ShapeDtypeStruct(start.shape, f32), jax.ShapeDtypeStruct((own, 2, width), f32)],
        in_specs=[pl.BlockSpec(memory_space=pltpu.SMEM)] + [in_vmem] * 4,
        scratch_shapes=[pltpu.VMEM((2 * width, 2 * width), f32)] + [pltpu.VMEM((rows, width), f32)] * 2,
    )(col.reshape(1), *(pltpu.with_memory_space_constraint(x, pltpu.VMEM) for x in (terms, other, col_terms, start)))


def shards(kron_inverse, activations):
    rows, cols = kron_inverse.shape
    blocks, width = activations.shape[:2]
    wide = blocks * width
    planes = lax.axis_size("row")
    devices = lax.axis_size("col")
    depth = devices // 2
    along = list(range(depth))
    around = [seat // 2 + seat % 2 * (planes // 2) for seat in range(planes)]
    seats = [around.index(z) for z in along]
    row = lax.axis_index("row")
    row = row % (planes // 2) * 2 + row // (planes // 2)
    col = lax.axis_index("col")
    lines = [[2 * z + k for z in along] for k in range(2)]

    def from_partner(value):
        return lax.ppermute(value, "col", [(at, at ^ 1) for at in range(devices)])

    def over_z(value):
        return lax.all_to_all(value, "col", 0, 0, tiled=True, axis_index_groups=lines)

    def over_plane(value):
        return lax.all_to_all(value, "row", 0, 0, tiled=True, axis_index_groups=[around])

    half = rows // 2
    share = half // depth
    slab = wide // planes

    def whole(value):
        left = value[:, :share].reshape(half, width)
        return jnp.concatenate([left, value[:, share:].reshape(half, width)], axis=1)

    send, start, turned = loading(col, kron_inverse.T, activations.transpose(0, 2, 1))
    summed = keeping(col, start, turned) + from_partner(send)
    groups = width // slab
    mine = lax.dynamic_slice(turned, (row // groups, 0, row % groups * slab), (1, cols, slab))
    mine = jnp.pad(mine.reshape(depth, share, slab), ((0, 0), (0, -share % groups), (0, 0)))
    mine = jnp.flip(mine.reshape(depth, -1, groups, slab), 2).reshape(depth, -1, width)
    parts = [summed[at].reshape(depth, share, width) for at in range(blocks)]
    got = over_z(jnp.concatenate([*parts, mine], axis=1))
    held = blocks * share
    level = over_plane(spread(got, planes, held))
    cut = held // planes
    rest = held % planes
    turns = depth // rest
    line = over_z(slab_terms(row, got, level, seats))
    send, row_half = plane_terms(row, line, slab + depth * cut + turns + 1, slab, held)
    disc = over_plane(send)
    terms = jnp.concatenate([disc[:, :slab].reshape(wide, width), disc[:, -1], row_half], axis=0)
    other = from_partner(terms)
    part = disc[:, slab : slab + depth * cut].reshape(planes, depth, cut, width)
    part = part.transpose(1, 0, 2, 3).reshape(depth, planes * cut, width)
    spare = disc[:, slab + depth * cut : -1].reshape(-1, rest, turns, width)
    spare = spare.transpose(0, 2, 1, 3).reshape(depth, rest, width)
    col_terms = whole(jnp.concatenate([part, spare], axis=1))
    updated, gains = closing(col, terms, other, col_terms, start, rows // devices)
    return updated.T, gains.transpose(1, 0, 2)


def solution(mesh):
    return jax.shard_map(
        shards,
        mesh=mesh,
        in_specs=(P("row", "col"), P(None, None, "col")),
        out_specs=(P("row", "col"), P(None, ("row", "col"), None)),
        check_vma=False,
    )
```

```python
import functools

import jax
import jax.numpy as jnp
from jax import lax
from jax.experimental import pallas as pl
from jax.experimental.pallas import tpu as pltpu
from jax.sharding import PartitionSpec as P

highest = lax.Precision.HIGHEST
f32 = jnp.float32


def dot(a, b, dims=((1,), (0,))):
    return lax.dot_general(a, b, (dims, ((), ())), precision=highest, preferred_element_type=f32)


def rough(a, b):
    return jnp.dot(a.astype(jnp.bfloat16), b.astype(jnp.bfloat16), preferred_element_type=f32)


def unit(size):
    rows = lax.broadcasted_iota(jnp.int32, (size, size), 0)
    return (rows == lax.broadcasted_iota(jnp.int32, (size, size), 1)).astype(f32)


def expanded(block):
    eye = unit(block.shape[0])
    scale_col = lax.rsqrt(jnp.sum(block * eye, axis=1, keepdims=True))
    scale_row = lax.rsqrt(jnp.sum(block * eye, axis=0, keepdims=True))
    scaled = block * scale_col * scale_row
    off = scaled - eye
    square = rough(off, off)
    spread = jnp.sum(jnp.sum(square * square, axis=0, keepdims=True), axis=1, keepdims=True)
    step = jnp.minimum(1.0, 1.9 / (1.0 + jnp.sqrt(jnp.sqrt(spread))))
    rest = (1.0 - step) * eye - step * off
    guess = eye + rest
    rest = (1.0 - step) * (rest - step * off) + step * step * square
    for turn in range(2):
        more = rough(guess, rest)
        if turn < 1:
            rest = rough(rest, rest)
        guess = guess + more
    guess = guess * step
    rest = eye - dot(guess, scaled)
    miss = jnp.sum(rest * rest)
    guess = guess + rough(rest, guess)
    rest = eye - dot(guess, scaled)
    return (guess + rough(rest, guess)) * scale_col * scale_row, miss


def eliminated(block, work_ref):
    size = block.shape[0]
    lane = lax.broadcasted_iota(jnp.int32, (1, size), 1)
    line = lax.broadcasted_iota(jnp.int32, (size, 1), 0)
    work_ref[:size, :size] = block

    def sweep(at, carry):
        value = work_ref[:size, :size]
        row = jnp.sum(jnp.where(line == at, value, 0.0), axis=0, keepdims=True)
        here = lane == at
        col = jnp.sum(jnp.where(here, value, 0.0), axis=1, keepdims=True)
        pivot = 1.0 / jnp.sum(jnp.where(here, row, 0.0), axis=1, keepdims=True)
        row = jnp.where(here, pivot, row * pivot)
        col = jnp.where(line == at, 0.0, col)
        value = jnp.where(here, 0.0, value)
        work_ref[:size, :size] = jnp.where(line == at, row, value - col * row)
        return carry

    lax.fori_loop(0, size, sweep, 0)
    guess = work_ref[:size, :size]
    return guess + dot(unit(size) - dot(guess, block), guess)


def product(high, start_ref, lines_ref, out_ref):
    blocks, half, width = out_ref.shape
    lines = jnp.concatenate([lines_ref[at] for at in range(blocks)], axis=1)

    def store(first):
        value = dot(start_ref[:, first : first + half], lines, ((0,), (0,)))
        for at in range(blocks):
            out_ref[at] = value[:, at * width : (at + 1) * width]

    pl.when(high == 0)(lambda: store(0))
    pl.when(high != 0)(lambda: store(half))


def loading_kernel(col_ref, far_start_ref, far_lines_ref, send_ref, start_ref, lines_ref, done_ref):
    moves = (
        pltpu.make_async_copy(far_start_ref, start_ref, done_ref.at[0]),
        pltpu.make_async_copy(far_lines_ref, lines_ref, done_ref.at[1]),
    )
    for move in moves:
        move.start()
    for move in moves:
        move.wait()
    product(1 - lax.rem(col_ref[0], 2), start_ref, lines_ref, send_ref)


def loading(col, start, lines):
    blocks, _, width = lines.shape
    in_hbm = pl.BlockSpec(memory_space=pl.ANY)
    return pl.pallas_call(
        loading_kernel,
        out_shape=[
            pltpu.VMEM((blocks, start.shape[1] // 2, width), f32),
            pltpu.VMEM(start.shape, f32),
            pltpu.VMEM(lines.shape, f32),
        ],
        in_specs=[pl.BlockSpec(memory_space=pltpu.SMEM), in_hbm, in_hbm],
        scratch_shapes=[pltpu.SemaphoreType.DMA((2,))],
    )(col.reshape(1), start, lines)


def keeping_kernel(col_ref, start_ref, lines_ref, out_ref):
    product(lax.rem(col_ref[0], 2), start_ref, lines_ref, out_ref)


def keeping(col, start, lines):
    blocks, _, width = lines.shape
    in_vmem = pl.BlockSpec(memory_space=pltpu.VMEM)
    return pl.pallas_call(
        keeping_kernel,
        out_shape=pltpu.VMEM((blocks, start.shape[1] // 2, width), f32),
        in_specs=[pl.BlockSpec(memory_space=pltpu.SMEM), in_vmem, in_vmem],
    )(col.reshape(1), *(pltpu.with_memory_space_constraint(x, pltpu.VMEM) for x in (start, lines)))


def spread_kernel(got_ref, out_ref):
    piece = jnp.sum(got_ref[:, : out_ref.shape[1]], axis=0)
    for at in range(out_ref.shape[0]):
        out_ref[at] = piece


def spread(got, planes, held):
    return pl.pallas_call(
        spread_kernel,
        out_shape=pltpu.VMEM((planes, held, got.shape[2]), f32),
        in_specs=[pl.BlockSpec(memory_space=pltpu.VMEM)],
    )(pltpu.with_memory_space_constraint(got, pltpu.VMEM))


def slab_kernel(row_ref, got_ref, level_ref, send_ref, right_ref, *, seats):
    depth, held, width = level_ref.shape
    share = held // 2
    tall = right_ref.shape[1]
    row = row_ref[0]
    slab = 2 * width // depth
    groups = width // slab
    packed = got_ref[:, held : held + tall // groups, :]
    packed = jnp.broadcast_to(packed[:, :, None, :], (depth, tall // groups, groups, width))
    packed = pltpu.roll(packed.reshape(depth * tall, width), slab, 1, stride=slab, stride_axis=0)
    right_ref[...] = jnp.zeros(right_ref.shape, f32)
    for at, seat in enumerate(seats):
        right_ref[at, :share, :width] = level_ref[seat, :share, :]
        right_ref[at, :share, width:] = level_ref[seat, share:, :]
    terms = dot(packed[:, :slab], right_ref[...].reshape(depth * tall, 2 * width), ((0,), (0,)))
    terms = pltpu.roll(terms, jnp.where(row == 0, 0, 2 * width - slab * row), 1)
    lane = lax.broadcasted_iota(jnp.int32, (slab, width), 1)
    block = jnp.where(lane < slab, terms[:, width:], 0.0)
    turned = jnp.concatenate([block, jnp.zeros((width - slab, width), f32)], axis=0).T
    block = jnp.where(row < depth // 2, block[: slab // 2], turned[slab // 2 : slab])
    block = jnp.concatenate([block[at : at + 1] for at in reversed(range(slab // 2))], axis=0)
    block = jnp.sum(pltpu.roll(block, 0, 1, stride=slab, stride_axis=0), axis=0, keepdims=True)
    piece = level_ref[row]
    cut = held // depth
    rest = held % depth
    part = level_ref[:, pl.ds(cut * row, cut), :]
    spare = level_ref[:, pl.ds(cut * depth + lax.rem(row, rest), 1), :]
    for at, seat in enumerate(seats):
        send_ref[at, :slab] = terms[:, :width]
        send_ref[at, slab : slab + held] = piece
        send_ref[at, slab + held : slab + held + cut] = part[seat]
        send_ref[at, slab + held + cut : slab + held + cut + 1] = spare[seat]
        send_ref[at, slab + held + cut + 1 :] = block


def slab_terms(row, got, level, seats):
    depth, held, width = level.shape
    cut = held // depth
    slab = 2 * width // depth
    tall = -(-held // 2 // 8) * 8
    in_vmem = pl.BlockSpec(memory_space=pltpu.VMEM)
    return pl.pallas_call(
        functools.partial(slab_kernel, seats=seats),
        out_shape=pltpu.VMEM((depth, slab + held + cut + 2, width), f32),
        in_specs=[pl.BlockSpec(memory_space=pltpu.SMEM), in_vmem, in_vmem],
        scratch_shapes=[pltpu.VMEM((depth, tall, 2 * width), f32)],
    )(row.reshape(1), *(pltpu.with_memory_space_constraint(x, pltpu.VMEM) for x in (got, level)))


def plane_kernel(row_ref, line_ref, send_ref, rows_ref, *, slab):
    planes, rows, _ = send_ref.shape
    depth, tall, width = line_ref.shape
    cut, turns = divmod(rows - slab - 1, depth)
    terms = jnp.sum(line_ref[:, :slab], axis=0)
    far = jnp.sum(line_ref[:, tall - 1 :], axis=0)
    spare = line_ref[pl.ds(row_ref[0] // (depth // turns) * turns, turns), tall - 2]
    half = rows_ref.shape[0] // 2
    share = half // depth
    for z in range(depth):
        rows_ref[z * share : (z + 1) * share] = line_ref[z, slab : slab + share]
        rows_ref[half + z * share : half + (z + 1) * share] = line_ref[z, slab + share : slab + 2 * share]
    for at in range(planes):
        send_ref[at, :slab] = terms
        for z in range(depth):
            first = slab + z * cut
            send_ref[at, first : first + cut] = line_ref[z, tall - 2 - cut : tall - 2]
        send_ref[at, rows - 1 - turns : rows - 1] = spare
        send_ref[at, rows - 1 :] = far


def plane_terms(row, line, rows, slab, held):
    planes, _, width = line.shape
    return pl.pallas_call(
        functools.partial(plane_kernel, slab=slab),
        out_shape=[pltpu.VMEM((planes, rows, width), f32), pltpu.VMEM((planes * held, width), f32)],
        in_specs=[pl.BlockSpec(memory_space=pltpu.SMEM), pl.BlockSpec(memory_space=pltpu.VMEM)],
    )(row.reshape(1), pltpu.with_memory_space_constraint(line, pltpu.VMEM))


def closing_kernel(col_ref, mine_ref, other_ref, cols_ref, start_ref, out_ref, gain_ref, work_ref, left_ref, right_ref):
    width = work_ref.shape[0] // 2
    half = left_ref.shape[0] // 2
    small = mine_ref.shape[0] - 2 * half
    slab = small - 2 * width
    groups = width // slab
    terms = mine_ref[:small] + other_ref[:small]

    core = lax.rem(col_ref[0], 2)
    for at, part_ref in ((core, mine_ref), (1 - core, other_ref)):
        at = pl.ds(pl.multiple_of(at * half, 8), half)
        left_ref[at] = part_ref[small : small + half]
        right_ref[at] = part_ref[small + half :]
    own = pl.ds(col_ref[0] * gain_ref.shape[0], gain_ref.shape[0])

    far = [terms[2 * width + n + m : 2 * width + n + m + 1] for n in range(groups) for m in (0, groups)]
    far = jnp.concatenate([jnp.broadcast_to(part, (slab // 2, width)) for part in far], axis=0)
    far = pltpu.roll(far, slab, 1, stride=slab, stride_axis=0)

    def stepped(value):
        parts = [value[n * slab : (n + 1) * slab] for n in range(groups)]
        return jnp.concatenate([pltpu.roll(part, n * slab, 1) if n else part for n, part in enumerate(parts)], axis=0)

    across = lax.broadcasted_iota(jnp.int32, (width, width), 1) // slab
    down = lax.broadcasted_iota(jnp.int32, (width, width), 0) // slab
    upper, lower, far = stepped(terms[:width]), stepped(terms[width : 2 * width]), stepped(far)
    upper_turned, lower_turned = upper.T, lower.T
    cross = jnp.where(across < down, upper, jnp.where(across > down, lower_turned, far))
    upper = jnp.where(across >= down, upper, upper_turned) + unit(width)
    lower = jnp.where(across >= down, lower, lower_turned) + unit(width)

    top = jnp.concatenate([upper, cross], axis=1)
    system = jnp.concatenate([top, jnp.concatenate([cross.T, lower], axis=1)], axis=0)

    def solve(inverse):
        first, miss = inverse(upper)
        full, more = inverse(system)
        gain_ref[:, 0] = dot(left_ref[own], first)
        gain_ref[:, 1] = dot(jnp.concatenate([left_ref[own], right_ref[own]], axis=1), full[:, width:])
        rows = jnp.concatenate([left_ref[...], right_ref[...]], axis=1)
        out_ref[...] = start_ref[...] - dot(dot(cols_ref[...], full), rows, ((1,), (1,)))
        return miss + more

    miss = solve(expanded)

    @pl.when(jnp.logical_not(miss < 1e-2))
    def _():
        solve(lambda value: (eliminated(value, work_ref), 0.0))


def closing(col, terms, other, col_terms, start, own):
    cols, rows = start.shape
    width = terms.shape[1]
    in_vmem = pl.BlockSpec(memory_space=pltpu.VMEM)
    return pl.pallas_call(
        closing_kernel,
        out_shape=[jax.ShapeDtypeStruct(start.shape, f32), jax.ShapeDtypeStruct((own, 2, width), f32)],
        in_specs=[pl.BlockSpec(memory_space=pltpu.SMEM)] + [in_vmem] * 4,
        scratch_shapes=[pltpu.VMEM((2 * width, 2 * width), f32)] + [pltpu.VMEM((rows, width), f32)] * 2,
    )(col.reshape(1), *(pltpu.with_memory_space_constraint(x, pltpu.VMEM) for x in (terms, other, col_terms, start)))


def shards(kron_inverse, activations):
    rows, cols = kron_inverse.shape
    blocks, width = activations.shape[:2]
    wide = blocks * width
    planes = lax.axis_size("row")
    devices = lax.axis_size("col")
    depth = devices // 2
    along = list(range(depth))
    around = [2, 11, 3, 10, 0, 4, 7, 5, 14, 12, 6, 9, 13, 8, 1, 15]
    around = [at for at in around if at < planes] + list(range(len(around), planes))
    seats = [around.index(z) for z in along]
    row = lax.axis_index("row")
    row = sum(jnp.where(row == at, seat, 0) for seat, at in enumerate(around))
    col = lax.axis_index("col")
    lines = [[2 * z + k for z in along] for k in range(2)]

    def from_partner(value):
        return lax.ppermute(value, "col", [(at, at ^ 1) for at in range(devices)])

    def over_z(value):
        return lax.all_to_all(value, "col", 0, 0, tiled=True, axis_index_groups=lines)

    def over_plane(value):
        return lax.all_to_all(value, "row", 0, 0, tiled=True, axis_index_groups=[around])

    half = rows // 2
    share = half // depth
    slab = wide // planes

    def whole(value):
        left = value[:, :share].reshape(half, width)
        return jnp.concatenate([left, value[:, share:].reshape(half, width)], axis=1)

    send, start, turned = loading(col, kron_inverse.T, activations.transpose(0, 2, 1))
    summed = keeping(col, start, turned) + from_partner(send)
    groups = width // slab
    mine = lax.dynamic_slice(turned, (row // groups, 0, row % groups * slab), (1, cols, slab))
    mine = jnp.pad(mine.reshape(depth, share, slab), ((0, 0), (0, -share % groups), (0, 0)))
    mine = jnp.flip(mine.reshape(depth, -1, groups, slab), 2).reshape(depth, -1, width)
    parts = [summed[at].reshape(depth, share, width) for at in range(blocks)]
    got = over_z(jnp.concatenate([*parts, mine], axis=1))
    held = blocks * share
    level = over_plane(spread(got, planes, held))
    cut = held // planes
    rest = held % planes
    turns = depth // rest
    line = over_z(slab_terms(row, got, level, seats))
    send, row_half = plane_terms(row, line, slab + depth * cut + turns + 1, slab, held)
    disc = over_plane(send)
    terms = jnp.concatenate([disc[:, :slab].reshape(wide, width), disc[:, -1], row_half], axis=0)
    other = from_partner(terms)
    part = disc[:, slab : slab + depth * cut].reshape(planes, depth, cut, width)
    part = part.transpose(1, 0, 2, 3).reshape(depth, planes * cut, width)
    spare = disc[:, slab + depth * cut : -1].reshape(-1, rest, turns, width)
    spare = spare.transpose(0, 2, 1, 3).reshape(depth, rest, width)
    col_terms = whole(jnp.concatenate([part, spare], axis=1))
    updated, gains = closing(col, terms, other, col_terms, start, rows // devices)
    return updated.T, gains.transpose(1, 0, 2)


def solution(mesh):
    return jax.shard_map(
        shards,
        mesh=mesh,
        in_specs=(P("row", "col"), P(None, None, "col")),
        out_specs=(P("row", "col"), P(None, ("row", "col"), None)),
        check_vma=False,
    )
```

```python
import functools

import jax
import jax.numpy as jnp
from jax import lax
from jax.experimental import pallas as pl
from jax.experimental.pallas import tpu as pltpu
from jax.sharding import PartitionSpec as P

highest = lax.Precision.HIGHEST
f32 = jnp.float32


def dot(a, b, dims=((1,), (0,))):
    return lax.dot_general(a, b, (dims, ((), ())), precision=highest, preferred_element_type=f32)


def rough(a, b):
    return jnp.dot(a.astype(jnp.bfloat16), b.astype(jnp.bfloat16), preferred_element_type=f32)


def unit(size):
    rows = lax.broadcasted_iota(jnp.int32, (size, size), 0)
    return (rows == lax.broadcasted_iota(jnp.int32, (size, size), 1)).astype(f32)


def expanded(block):
    eye = unit(block.shape[0])
    scale_col = lax.rsqrt(jnp.sum(block * eye, axis=1, keepdims=True))
    scale_row = lax.rsqrt(jnp.sum(block * eye, axis=0, keepdims=True))
    scaled = block * scale_col * scale_row
    off = scaled - eye
    square = rough(off, off)
    spread = jnp.sum(jnp.sum(square * square, axis=0, keepdims=True), axis=1, keepdims=True)
    step = jnp.minimum(1.0, 1.9 / (1.0 + jnp.sqrt(jnp.sqrt(spread))))
    rest = (1.0 - step) * eye - step * off
    guess = eye + rest
    rest = (1.0 - step) * (rest - step * off) + step * step * square
    for turn in range(2):
        more = rough(guess, rest)
        if turn < 1:
            rest = rough(rest, rest)
        guess = guess + more
    guess = guess * step
    rest = eye - dot(guess, scaled)
    miss = jnp.sum(rest * rest)
    guess = guess + rough(rest, guess)
    rest = eye - dot(guess, scaled)
    return (guess + rough(rest, guess)) * scale_col * scale_row, miss


def eliminated(block, work_ref):
    size = block.shape[0]
    lane = lax.broadcasted_iota(jnp.int32, (1, size), 1)
    line = lax.broadcasted_iota(jnp.int32, (size, 1), 0)
    work_ref[:size, :size] = block

    def sweep(at, carry):
        value = work_ref[:size, :size]
        row = jnp.sum(jnp.where(line == at, value, 0.0), axis=0, keepdims=True)
        here = lane == at
        col = jnp.sum(jnp.where(here, value, 0.0), axis=1, keepdims=True)
        pivot = 1.0 / jnp.sum(jnp.where(here, row, 0.0), axis=1, keepdims=True)
        row = jnp.where(here, pivot, row * pivot)
        col = jnp.where(line == at, 0.0, col)
        value = jnp.where(here, 0.0, value)
        work_ref[:size, :size] = jnp.where(line == at, row, value - col * row)
        return carry

    lax.fori_loop(0, size, sweep, 0)
    guess = work_ref[:size, :size]
    return guess + dot(unit(size) - dot(guess, block), guess)


def product(high, start_ref, lines_ref, out_ref):
    blocks, half, width = out_ref.shape
    lines = jnp.concatenate([lines_ref[at] for at in range(blocks)], axis=1)

    def store(first):
        value = dot(start_ref[:, first : first + half], lines, ((0,), (0,)))
        for at in range(blocks):
            out_ref[at] = value[:, at * width : (at + 1) * width]

    pl.when(high == 0)(lambda: store(0))
    pl.when(high != 0)(lambda: store(half))


def loading_kernel(col_ref, far_start_ref, far_lines_ref, send_ref, start_ref, lines_ref, done_ref):
    moves = (
        pltpu.make_async_copy(far_start_ref, start_ref, done_ref.at[0]),
        pltpu.make_async_copy(far_lines_ref, lines_ref, done_ref.at[1]),
    )
    for move in moves:
        move.start()
    for move in moves:
        move.wait()
    product(1 - lax.rem(col_ref[0], 2), start_ref, lines_ref, send_ref)


def loading(col, start, lines):
    blocks, _, width = lines.shape
    in_hbm = pl.BlockSpec(memory_space=pl.ANY)
    return pl.pallas_call(
        loading_kernel,
        out_shape=[
            pltpu.VMEM((blocks, start.shape[1] // 2, width), f32),
            pltpu.VMEM(start.shape, f32),
            pltpu.VMEM(lines.shape, f32),
        ],
        in_specs=[pl.BlockSpec(memory_space=pltpu.SMEM), in_hbm, in_hbm],
        scratch_shapes=[pltpu.SemaphoreType.DMA((2,))],
    )(col.reshape(1), start, lines)


def keeping_kernel(col_ref, start_ref, lines_ref, out_ref):
    product(lax.rem(col_ref[0], 2), start_ref, lines_ref, out_ref)


def keeping(col, start, lines):
    blocks, _, width = lines.shape
    in_vmem = pl.BlockSpec(memory_space=pltpu.VMEM)
    return pl.pallas_call(
        keeping_kernel,
        out_shape=pltpu.VMEM((blocks, start.shape[1] // 2, width), f32),
        in_specs=[pl.BlockSpec(memory_space=pltpu.SMEM), in_vmem, in_vmem],
    )(col.reshape(1), *(pltpu.with_memory_space_constraint(x, pltpu.VMEM) for x in (start, lines)))


def spread_kernel(got_ref, out_ref):
    piece = jnp.sum(got_ref[:, : out_ref.shape[1]], axis=0)
    for at in range(out_ref.shape[0]):
        out_ref[at] = piece


def spread(got, planes, held):
    return pl.pallas_call(
        spread_kernel,
        out_shape=pltpu.VMEM((planes, held, got.shape[2]), f32),
        in_specs=[pl.BlockSpec(memory_space=pltpu.VMEM)],
    )(pltpu.with_memory_space_constraint(got, pltpu.VMEM))


def slab_kernel(row_ref, got_ref, level_ref, send_ref, right_ref, *, seats):
    depth, held, width = level_ref.shape
    share = held // 2
    tall = right_ref.shape[1]
    row = row_ref[0]
    slab = 2 * width // depth
    groups = width // slab
    packed = got_ref[:, held : held + tall // groups, :]
    packed = jnp.broadcast_to(packed[:, :, None, :], (depth, tall // groups, groups, width))
    packed = pltpu.roll(packed.reshape(depth * tall, width), slab, 1, stride=slab, stride_axis=0)
    right_ref[...] = jnp.zeros(right_ref.shape, f32)
    for at, seat in enumerate(seats):
        right_ref[at, :share, :width] = level_ref[seat, :share, :]
        right_ref[at, :share, width:] = level_ref[seat, share:, :]
    terms = dot(packed[:, :slab], right_ref[...].reshape(depth * tall, 2 * width), ((0,), (0,)))
    terms = pltpu.roll(terms, jnp.where(row == 0, 0, 2 * width - slab * row), 1)
    lane = lax.broadcasted_iota(jnp.int32, (slab, width), 1)
    block = jnp.where(lane < slab, terms[:, width:], 0.0)
    turned = jnp.concatenate([block, jnp.zeros((width - slab, width), f32)], axis=0).T
    block = jnp.where(row < depth // 2, block[: slab // 2], turned[slab // 2 : slab])
    block = jnp.concatenate([block[at : at + 1] for at in reversed(range(slab // 2))], axis=0)
    block = jnp.sum(pltpu.roll(block, 0, 1, stride=slab, stride_axis=0), axis=0, keepdims=True)
    piece = level_ref[row]
    cut = held // depth
    rest = held % depth
    part = level_ref[:, pl.ds(cut * row, cut), :]
    spare = level_ref[:, pl.ds(cut * depth + lax.rem(row, rest), 1), :]
    for at, seat in enumerate(seats):
        send_ref[at, :slab] = terms[:, :width]
        send_ref[at, slab : slab + held] = piece
        send_ref[at, slab + held : slab + held + cut] = part[seat]
        send_ref[at, slab + held + cut : slab + held + cut + 1] = spare[seat]
        send_ref[at, slab + held + cut + 1 :] = block


def slab_terms(row, got, level, seats):
    depth, held, width = level.shape
    cut = held // depth
    slab = 2 * width // depth
    tall = -(-held // 2 // 8) * 8
    in_vmem = pl.BlockSpec(memory_space=pltpu.VMEM)
    return pl.pallas_call(
        functools.partial(slab_kernel, seats=seats),
        out_shape=pltpu.VMEM((depth, slab + held + cut + 2, width), f32),
        in_specs=[pl.BlockSpec(memory_space=pltpu.SMEM), in_vmem, in_vmem],
        scratch_shapes=[pltpu.VMEM((depth, tall, 2 * width), f32)],
    )(row.reshape(1), *(pltpu.with_memory_space_constraint(x, pltpu.VMEM) for x in (got, level)))


def plane_kernel(row_ref, line_ref, send_ref, rows_ref, *, slab):
    planes, rows, _ = send_ref.shape
    depth, tall, width = line_ref.shape
    cut, turns = divmod(rows - slab - 1, depth)
    terms = jnp.sum(line_ref[:, :slab], axis=0)
    far = jnp.sum(line_ref[:, tall - 1 :], axis=0)
    spare = line_ref[pl.ds(row_ref[0] // (depth // turns) * turns, turns), tall - 2]
    half = rows_ref.shape[0] // 2
    share = half // depth
    for z in range(depth):
        rows_ref[z * share : (z + 1) * share] = line_ref[z, slab : slab + share]
        rows_ref[half + z * share : half + (z + 1) * share] = line_ref[z, slab + share : slab + 2 * share]
    for at in range(planes):
        send_ref[at, :slab] = terms
        for z in range(depth):
            first = slab + z * cut
            send_ref[at, first : first + cut] = line_ref[z, tall - 2 - cut : tall - 2]
        send_ref[at, rows - 1 - turns : rows - 1] = spare
        send_ref[at, rows - 1 :] = far


def plane_terms(row, line, rows, slab, held):
    planes, _, width = line.shape
    return pl.pallas_call(
        functools.partial(plane_kernel, slab=slab),
        out_shape=[pltpu.VMEM((planes, rows, width), f32), pltpu.VMEM((planes * held, width), f32)],
        in_specs=[pl.BlockSpec(memory_space=pltpu.SMEM), pl.BlockSpec(memory_space=pltpu.VMEM)],
    )(row.reshape(1), pltpu.with_memory_space_constraint(line, pltpu.VMEM))


def closing_kernel(col_ref, mine_ref, other_ref, cols_ref, start_ref, out_ref, gain_ref, work_ref, left_ref, right_ref):
    width = work_ref.shape[0] // 2
    half = left_ref.shape[0] // 2
    small = mine_ref.shape[0] - 2 * half
    slab = small - 2 * width
    groups = width // slab
    terms = mine_ref[:small] + other_ref[:small]

    core = lax.rem(col_ref[0], 2)
    for at, part_ref in ((core, mine_ref), (1 - core, other_ref)):
        at = pl.ds(pl.multiple_of(at * half, 8), half)
        left_ref[at] = part_ref[small : small + half]
        right_ref[at] = part_ref[small + half :]
    own = pl.ds(col_ref[0] * gain_ref.shape[0], gain_ref.shape[0])

    far = [terms[2 * width + n + m : 2 * width + n + m + 1] for n in range(groups) for m in (0, groups)]
    far = jnp.concatenate([jnp.broadcast_to(part, (slab // 2, width)) for part in far], axis=0)
    far = pltpu.roll(far, slab, 1, stride=slab, stride_axis=0)

    def stepped(value):
        parts = [value[n * slab : (n + 1) * slab] for n in range(groups)]
        return jnp.concatenate([pltpu.roll(part, n * slab, 1) if n else part for n, part in enumerate(parts)], axis=0)

    across = lax.broadcasted_iota(jnp.int32, (width, width), 1) // slab
    down = lax.broadcasted_iota(jnp.int32, (width, width), 0) // slab
    upper, lower, far = stepped(terms[:width]), stepped(terms[width : 2 * width]), stepped(far)
    upper_turned, lower_turned = upper.T, lower.T
    cross = jnp.where(across < down, upper, jnp.where(across > down, lower_turned, far))
    upper = jnp.where(across >= down, upper, upper_turned) + unit(width)
    lower = jnp.where(across >= down, lower, lower_turned) + unit(width)

    top = jnp.concatenate([upper, cross], axis=1)
    system = jnp.concatenate([top, jnp.concatenate([cross.T, lower], axis=1)], axis=0)

    def solve(inverse):
        first, miss = inverse(upper)
        full, more = inverse(system)
        gain_ref[:, 0] = dot(left_ref[own], first)
        gain_ref[:, 1] = dot(jnp.concatenate([left_ref[own], right_ref[own]], axis=1), full[:, width:])
        rows = jnp.concatenate([left_ref[...], right_ref[...]], axis=1)
        out_ref[...] = start_ref[...] - dot(dot(cols_ref[...], full), rows, ((1,), (1,)))
        return miss + more

    miss = solve(expanded)

    @pl.when(jnp.logical_not(miss < 1e-2))
    def _():
        solve(lambda value: (eliminated(value, work_ref), 0.0))


def closing(col, terms, other, col_terms, start, own):
    cols, rows = start.shape
    width = terms.shape[1]
    in_vmem = pl.BlockSpec(memory_space=pltpu.VMEM)
    return pl.pallas_call(
        closing_kernel,
        out_shape=[jax.ShapeDtypeStruct(start.shape, f32), jax.ShapeDtypeStruct((own, 2, width), f32)],
        in_specs=[pl.BlockSpec(memory_space=pltpu.SMEM)] + [in_vmem] * 4,
        scratch_shapes=[pltpu.VMEM((2 * width, 2 * width), f32)] + [pltpu.VMEM((rows, width), f32)] * 2,
    )(col.reshape(1), *(pltpu.with_memory_space_constraint(x, pltpu.VMEM) for x in (terms, other, col_terms, start)))


def shards(kron_inverse, activations):
    rows, cols = kron_inverse.shape
    blocks, width = activations.shape[:2]
    wide = blocks * width
    planes = lax.axis_size("row")
    devices = lax.axis_size("col")
    depth = devices // 2
    along = list(range(depth))
    around = [1, 12, 11, 4, 9, 7, 3, 14, 2, 10, 15, 5, 6, 0, 13, 8]
    around = [at for at in around if at < planes] + list(range(len(around), planes))
    seats = [around.index(z) for z in along]
    row = lax.axis_index("row")
    row = sum(jnp.where(row == at, seat, 0) for seat, at in enumerate(around))
    col = lax.axis_index("col")
    lines = [[2 * z + k for z in along] for k in range(2)]

    def from_partner(value):
        return lax.ppermute(value, "col", [(at, at ^ 1) for at in range(devices)])

    def over_z(value):
        return lax.all_to_all(value, "col", 0, 0, tiled=True, axis_index_groups=lines)

    def over_plane(value):
        return lax.all_to_all(value, "row", 0, 0, tiled=True, axis_index_groups=[around])

    half = rows // 2
    share = half // depth
    slab = wide // planes

    def whole(value):
        left = value[:, :share].reshape(half, width)
        return jnp.concatenate([left, value[:, share:].reshape(half, width)], axis=1)

    send, start, turned = loading(col, kron_inverse.T, activations.transpose(0, 2, 1))
    summed = keeping(col, start, turned) + from_partner(send)
    groups = width // slab
    mine = lax.dynamic_slice(turned, (row // groups, 0, row % groups * slab), (1, cols, slab))
    mine = jnp.pad(mine.reshape(depth, share, slab), ((0, 0), (0, -share % groups), (0, 0)))
    mine = jnp.flip(mine.reshape(depth, -1, groups, slab), 2).reshape(depth, -1, width)
    parts = [summed[at].reshape(depth, share, width) for at in range(blocks)]
    got = over_z(jnp.concatenate([*parts, mine], axis=1))
    held = blocks * share
    level = over_plane(spread(got, planes, held))
    cut = held // planes
    rest = held % planes
    turns = depth // rest
    line = over_z(slab_terms(row, got, level, seats))
    send, row_half = plane_terms(row, line, slab + depth * cut + turns + 1, slab, held)
    disc = over_plane(send)
    terms = jnp.concatenate([disc[:, :slab].reshape(wide, width), disc[:, -1], row_half], axis=0)
    other = from_partner(terms)
    part = disc[:, slab : slab + depth * cut].reshape(planes, depth, cut, width)
    part = part.transpose(1, 0, 2, 3).reshape(depth, planes * cut, width)
    spare = disc[:, slab + depth * cut : -1].reshape(-1, rest, turns, width)
    spare = spare.transpose(0, 2, 1, 3).reshape(depth, rest, width)
    col_terms = whole(jnp.concatenate([part, spare], axis=1))
    updated, gains = closing(col, terms, other, col_terms, start, rows // devices)
    return updated.T, gains.transpose(1, 0, 2)


def solution(mesh):
    return jax.shard_map(
        shards,
        mesh=mesh,
        in_specs=(P("row", "col"), P(None, None, "col")),
        out_specs=(P("row", "col"), P(None, ("row", "col"), None)),
        check_vma=False,
    )
```
